128 devices in a mesh: phase: 4 (over z), vox: 32 (over x, y, core).
Axes of the slice: x: 4, y: 4, z: 4, core: 2. Of those that a mesh axis runs over, the one named last changes fastest.
Arguments:
- influence: float32 [4, 65536, 1536], P('phase', 'vox'), may hold values from -0.15625 to 0.15625
- weights: float32 [1536, 128], P(('phase', 'vox')), may hold values from 0.5 to 2
- warp_tiles: float32 [64, 128, 128], replicated, may hold values from -0.5 to 0.5
- owners: int32 [4, 512, 1], P('phase', 'vox'), may hold values from 0 to 31; in each aligned block of 16 rows (0 to 15, 16 to 31, ..., all dimensions but the last counted through in order) at most 2 rows name the same one
- owner_slot: int32 [4, 512], P('phase', 'vox'), may hold values from 0 to 15
- tile_index: int32 [4, 512], P('phase', 'vox'), may hold values from 0 to 63
- structure: int32 [65536], P('vox'), may hold values from 0 to 7
- prescribed: float32 [8, 128], replicated, may hold values from 0 to 3
- importance: float32 [8], replicated, may hold values from 0.25 to 4
- step_size: float32 [128], replicated, may hold values from 0.02 to 0.08
Outputs:
- new_weights: float32 [1536, 128], P(('phase', 'vox'))
- dose_field: float32 [65536, 128], P('vox')
The draws below stay inside these ranges and needn't reach their ends.
Inputs may be any that keep to these rules, and one draw needn't show every extreme that they name: `owners`: for each phase and each device of vox, at most 2 of that device's 16 blocks name one owner, and some device reaches 2.
All inputs are finite; a program needn't handle non-finite values.
Results may differ from the reference program's by a relative error of at most 0.00023.
Values sent between devices are 32-bit elements; how exact they have to be, the bound alone decides.
A program may use at most 128 MiB of HBM per device.

```python
import math
import jax
import jax.numpy as jnp
import numpy as np
from jax import lax

SPOTS = 1536
PLANS = 128
BLK = 128
CAP = 2
NTILE = 64
NSTRUCT = 8
ITERS = 2
PHASES = 4
VOXELS = 65536
BLK_DEV = 16
NBLK = 512
N_VOX = 32


def plant(entries, stream_key, least, high):
    longest = entries.shape.index(max(entries.shape))
    spots = []
    for shift in (0, 1):
        where = [jax.random.randint(jax.random.fold_in(stream_key, axis), (), 0, length) for axis, length in enumerate(entries.shape)]
        where[longest] = (where[longest] + shift) % entries.shape[longest]
        spots.append(tuple(where))
    return entries.at[spots[0]].set(least).at[spots[1]].set(high)


def shard_levels(own_key, dims, split, smallest, top_value):
    factor_of = 1.0
    for position, parts in split:
        heights = jax.random.uniform(jax.random.fold_in(jax.random.fold_in(own_key, 6), position), (parts,), jnp.float32, smallest / len(split), top_value / len(split))
        factor_of = factor_of * jnp.repeat(jnp.exp(heights), dims[position] // parts).reshape((-1,) + (1,) * (len(dims) - 1 - position))
    return factor_of


def deal_out(rng, own, number, rows, number_of, top, bound, skew):
    sequence = jax.random.permutation(rng, number_of)
    heavy_load, ordinary = load_shares(number_of, rows * top, bound, skew, True), load_shares(number_of, rows * top, bound, skew, False)
    places = jnp.arange(number_of)

    def named(lengths, offset_by):
        used = int((lengths > 0).sum())
        fixed = max(1, used // 4)
        passed = fixed + (places - fixed + offset_by * (used - fixed)) % max(1, number_of - fixed)
        return jnp.zeros((number_of,), jnp.int32).at[sequence[jnp.where(places < fixed, places, passed)]].set(jnp.asarray(lengths, jnp.int32))

    lengths = jnp.where(number % 4 == 0, named(heavy_load, number // 4), named(ordinary, number - number // 4 - 1))
    mixed = jax.random.permutation(jax.random.fold_in(own, 3), number_of)
    giver, sink = mixed[0:number_of // 2 * 2:2], mixed[1:number_of // 2 * 2:2]
    room = jnp.minimum(lengths[giver] - 1, bound - lengths[sink]) // 2
    room = jnp.where((giver == sequence[0]) | (sink == sequence[0]) | (lengths[sink] == 0), 0, jnp.maximum(room, 0))
    passed = jax.random.randint(jax.random.fold_in(own, 4), (number_of // 2,), 0, 1 << 20) % (room + 1)
    lengths = lengths.at[giver].add(-passed).at[sink].add(passed)
    labels = jnp.searchsorted(jnp.cumsum(lengths), jnp.arange(rows * top), side="right").astype(jnp.int32)
    grid = labels.reshape(top, rows).T
    grid = grid[jax.random.permutation(jax.random.fold_in(own, 1), rows)]
    offset_by = jax.random.randint(jax.random.fold_in(own, 2), (rows, 1), 0, top)
    return jnp.take_along_axis(grid, (jnp.arange(top)[None, :] + offset_by) % top, axis=1)


def load_shares(number_of, total, limit, lean, full):
    portions = [(1 << 20) // math.isqrt(rank ** lean) + 1 for rank in range(1, number_of + 1)]
    largest = limit if full else min(limit, max(-(-total // number_of), total * portions[0] // sum(portions)))
    least = 1 if total - largest >= number_of - 1 else 0
    given, surplus = [largest] + [least] * (number_of - 1), total - largest - least * (number_of - 1)
    while surplus > 0:
        movable = [i for i in range(1, number_of) if given[i] < largest] or [i for i in range(1, number_of) if given[i] < limit]
        mass, budget = sum([portions[i] for i in movable]), surplus
        for i in movable:
            addition = min(limit - given[i], max(1, budget * portions[i] // mass), surplus)
            given[i] = given[i] + addition
            surplus = surplus - addition
    return np.array(given)


def gaussian(key, extent, deviation, bound, cuts=(), kind=jnp.bfloat16):
    values = jax.random.normal(key, extent, jnp.float32) * deviation
    if len(cuts) > 0:
        values = shard_levels(key, extent, cuts, -0.22, 0.18) * values
    return jnp.clip(values, min=-bound, max=bound).astype(kind)


def setup_inputs(seed: int = 0) -> dict:
    keys = jax.random.split(jax.random.key(seed), 11)
    influence = gaussian(keys[0], (PHASES, VOXELS, SPOTS), SPOTS ** -0.5, 0.15625, ((0, 4), (1, 32)), jnp.float32)
    weights = jnp.clip(jnp.exp(math.log(2.0) - 1.3862944 * jax.random.uniform(keys[1], (SPOTS, PLANS), jnp.float32) ** shard_levels(keys[1], (SPOTS, PLANS), ((0, 128),), -0.2, 0.2)), 0.5, 2.0)
    warp_tiles = gaussian(keys[2], (NTILE, BLK, BLK), BLK ** -0.5, 0.5, (), jnp.float32)
    owners_keys = jax.random.split(jax.random.fold_in(keys[3], 1), PHASES * NBLK // BLK_DEV)
    owners_turns = jax.random.permutation(jax.random.fold_in(keys[3], 3), PHASES * NBLK // BLK_DEV)
    owners = jax.vmap(lambda own, number: deal_out(jax.random.fold_in(keys[3], 2), own, number, BLK_DEV, N_VOX, 1, CAP, 2))(owners_keys, owners_turns).reshape((PHASES, NBLK, 1))
    owner_slot = plant(jax.random.randint(keys[4], (PHASES, NBLK), 0, BLK_DEV), jax.random.fold_in(keys[4], 1), 0, BLK_DEV - 1).astype(jnp.int32)
    tile_index = plant(jax.random.randint(keys[5], (PHASES, NBLK), 0, NTILE), jax.random.fold_in(keys[5], 1), 0, NTILE - 1).astype(jnp.int32)
    structure = plant(jax.random.randint(keys[6], (VOXELS,), 0, NSTRUCT), jax.random.fold_in(keys[6], 1), 0, NSTRUCT - 1).astype(jnp.int32)
    prescribed = jnp.clip(jax.random.uniform(keys[7], (NSTRUCT, PLANS), jnp.float32, 0.0, 3.0), 0.0, 3.0)
    importance = jnp.clip(jnp.exp(jax.random.uniform(keys[8], (NSTRUCT,), jnp.float32, math.log(0.25), math.log(4.0))), 0.25, 4.0)
    step_size = jnp.clip(jnp.exp(jax.random.uniform(keys[9], (PLANS,), jnp.float32, math.log(0.02), math.log(0.08))), 0.02, 0.08)
    return dict(influence=influence, weights=weights, warp_tiles=warp_tiles, owners=owners, owner_slot=owner_slot, tile_index=tile_index, structure=structure, prescribed=prescribed, importance=importance, step_size=step_size)


def reference(influence, weights, warp_tiles, owners, owner_slot, tile_index, structure, prescribed, importance, step_size):
    highest = lax.Precision.HIGHEST
    num_blocks = VOXELS // BLK
    member = (structure[:, None] == jnp.arange(NSTRUCT, dtype=jnp.int32)[None, :]).astype(jnp.float32)
    target_dose = jnp.dot(member, prescribed, precision=highest, preferred_element_type=jnp.float32)
    voxel_weight = jnp.dot(member, importance[:, None], precision=highest, preferred_element_type=jnp.float32)
    new_weights = weights
    dose_field = jnp.zeros((VOXELS, PLANS), jnp.float32)
    for iteration in range(ITERS):
        summed = jnp.zeros((num_blocks, BLK, PLANS), jnp.float32)
        for phase_index in range(PHASES):
            phase_dose = jnp.dot(influence[phase_index], new_weights, precision=highest, preferred_element_type=jnp.float32)
            blocks = phase_dose.reshape(num_blocks, BLK, PLANS)
            chosen = warp_tiles[tile_index[phase_index]]
            warped = jnp.einsum("kab,kbp->kap", chosen, blocks, precision=highest)
            target = (owners[phase_index, :, 0] * BLK_DEV + owner_slot[phase_index]).astype(jnp.int32)
            summed = summed + jax.ops.segment_sum(warped, target, num_segments=num_blocks)
        dose_field = summed.reshape(VOXELS, PLANS)
        adjoint = voxel_weight * (dose_field - target_dose)
        adjoint_blocks = adjoint.reshape(num_blocks, BLK, PLANS)
        gradient = jnp.zeros((SPOTS, PLANS), jnp.float32)
        for phase_index in range(PHASES):
            chosen = warp_tiles[tile_index[phase_index]]
            target = (owners[phase_index, :, 0] * BLK_DEV + owner_slot[phase_index]).astype(jnp.int32)
            pulled = adjoint_blocks[target]
            local_adjoint = jnp.einsum("kab,kap->kbp", chosen, pulled, precision=highest).reshape(VOXELS, PLANS)
            gradient = gradient + jnp.dot(influence[phase_index].T, local_adjoint, precision=highest, preferred_element_type=jnp.float32)
        new_weights = jnp.maximum(new_weights - step_size[None, :] * gradient, 0.0)
    return new_weights, dose_field
```

```python
import jax
import jax.numpy as jnp
from jax import lax
from jax.experimental import pallas as pl
from jax.experimental.pallas import tpu as pltpu
from jax.sharding import Mesh
from jax.sharding import PartitionSpec as P

AXES = ("z", "x", "y", "c")
VOX = ("x", "y", "c")
SIZES = (4, 4, 4, 2)
NDEV = 128
NVOX = 32
NSTRUCT = 8
ITERS = 2
PLANS = 128
BLK = 128
BLOCKS = 16
CHUNKS = 2
PER = BLOCKS // CHUNKS
SPOTS = 1536
OWN = SPOTS // NDEV
ROWS = BLOCKS * BLK
TARGETS = NVOX * BLOCKS
SOURCES = NDEV * BLOCKS
NTILE = 64
LOAD = 256
GROUP = 512
LOGICAL = pl.DeviceIdType.LOGICAL
F32 = jnp.float32
BF16 = jnp.bfloat16


def offset_parts(offset):
    return offset // 32, (offset // 8) % 4, (offset // 2) % 4, offset % 2


def hops(offset):
    z, x, y, c = offset_parts(offset)
    return 2 * (min(z, 4 - z) + min(x, 4 - x) + min(y, 4 - y)) + c


OFFSETS = sorted(range(1, NDEV), key=lambda o: -hops(o))


def peers():
    z, x, y, c = [lax.axis_index(a) for a in AXES]
    pz = [lax.rem(z + d, 4) * 32 for d in range(4)]
    px = [lax.rem(x + d, 4) * 8 for d in range(4)]
    py = [lax.rem(y + d, 4) * 2 for d in range(4)]
    pc = [lax.rem(c + d, 2) for d in range(2)]
    zx = [[pz[a] + px[b] for b in range(4)] for a in range(4)]
    yc = [[py[a] + pc[b] for b in range(2)] for a in range(4)]

    def index(offset):
        dz, dx, dy, dc = offset_parts(offset)
        return zx[dz][dx] + yc[dy][dc]

    return index


def halves(value):
    high = value.astype(BF16)
    low = (value - high.astype(F32)).astype(BF16)
    return high, low


def dot(a, b):
    return jnp.dot(a, b, preferred_element_type=F32)


def joined(pair):
    return pair[:, :PLANS] + pair[:, PLANS:]


def kernel(
    tile_ids,
    importance,
    influence,
    weights,
    tiles,
    owners,
    slots,
    structure,
    prescribed,
    step,
    new_weights,
    dose_out,
    staged,
    mat_hi,
    mat_lo,
    tra_hi,
    tra_lo,
    tile_buf,
    warp,
    warp_t,
    info_out,
    info_in,
    gather_in,
    gather_t,
    w_buf,
    w_cat,
    w_own,
    w_next,
    out_buf,
    in_buf,
    in_cat,
    dose,
    target_dose,
    voxel_weight,
    adj_cat,
    back_buf,
    adj_buf,
    la_cat,
    grad,
    grad_in,
    field_out,
    field_in,
    load_sem,
    tile_sem,
    info_ss,
    info_rs,
    w_ss,
    w_rs,
    out_ss,
    out_rs,
    back_ss,
    back_rs,
    grad_ss,
    grad_rs,
    field_ss,
    field_rs,
):
    index = peers()
    me = index(0)
    vox_of = lambda device: lax.rem(device, NVOX)

    def send_all(src, dst, send_sem, recv_sem):
        for o in OFFSETS:
            to = index(o)
            pltpu.make_async_remote_copy(
                src_ref=src(to),
                dst_ref=dst,
                send_sem=send_sem,
                recv_sem=recv_sem,
                device_id=to,
                device_id_type=LOGICAL,
            ).start()
        pltpu.make_async_copy(src(me), dst, recv_sem).start()

    def wait(ref, sem):
        pltpu.make_async_copy(ref, ref, sem).wait()

    loads = []
    for n in range(ROWS // LOAD):
        loads.append(
            pltpu.make_async_copy(
                influence.at[0, pl.ds(n * LOAD, LOAD)], staged.at[n % 4], load_sem.at[n % 4]
            )
        )
    for n in range(4):
        loads[n].start()
    tile_load = pltpu.make_async_copy(tiles, tile_buf, tile_sem)
    tile_load.start()

    barrier = pltpu.get_barrier_semaphore()
    for o in OFFSETS:
        pl.semaphore_signal(barrier, inc=1, device_id=index(o), device_id_type=LOGICAL)

    info_out[...] = jnp.zeros((BLK, BLK), F32)
    info_out[BLOCKS : 2 * BLOCKS, :] = structure[...].astype(F32)
    turned = info_out[...].T
    w_next[0:1, 0:BLOCKS] = (slots[...] * NVOX + owners[...]).astype(F32)
    lane = lax.broadcasted_iota(jnp.int32, (BLK, BLK), 1)
    info_out[...] = jnp.where(lane < BLOCKS, w_next[0:1, :], turned)

    for n in range(ROWS // LOAD):
        loads[n].wait()

        @pl.loop(0, SPOTS // BLK)
        def _(k, n=n):
            cols = pl.ds(pl.multiple_of(k * BLK, BLK), BLK)
            for h in range(LOAD // BLK):
                part = staged[n % 4, h * BLK : (h + 1) * BLK, cols]
                rows = pl.ds(n * LOAD + h * BLK, BLK)
                high, low = halves(part)
                mat_hi[rows, cols] = high
                mat_lo[rows, cols] = low
                high, low = halves(part.T)
                tra_hi[cols, rows] = high
                tra_lo[cols, rows] = low

        if n + 4 < ROWS // LOAD:
            loads[n + 4].start()

    tile_load.wait()

    @pl.loop(0, BLOCKS)
    def _(b):
        tile = tile_buf[tile_ids[0, b]]
        high, low = halves(tile)
        warp[b, :, 0:BLK] = high
        warp[b, :, BLK : 2 * BLK] = low
        warp[b, :, 2 * BLK :] = high
        high, low = halves(tile.T)
        warp_t[b, :, 0:BLK] = high
        warp_t[b, :, BLK : 2 * BLK] = low
        warp_t[b, :, 2 * BLK :] = high

    w_own[...] = weights[...]
    pl.semaphore_wait(barrier, NDEV - 1)
    send_all(lambda to: weights, w_buf.at[0, pl.ds(me * OWN, OWN)], w_ss.at[0], w_rs.at[0])
    send_all(
        lambda to: info_out.at[pl.ds(to, 1)], info_in.at[pl.ds(me, 1)], info_ss, info_rs
    )

    def warped(matrix, value):
        high, low = halves(value)
        return dot(matrix, jnp.concatenate([high, high, low], axis=0))

    def tables():
        wait(info_in, info_rs)
        info = info_in[...]
        turned = info.T
        down = lax.broadcasted_iota(jnp.int32, (TARGETS, BLK), 0).astype(F32)
        across = lax.broadcasted_iota(jnp.int32, (BLK, TARGETS), 1).astype(F32)
        for b in range(BLOCKS):
            at = slice(b * BLK, (b + 1) * BLK)
            gather_in[:, at] = jnp.where(down == turned[b : b + 1, :], 1.0, 0.0).astype(BF16)
            gather_t[at, :] = jnp.where(across == info[:, b : b + 1], 1.0, 0.0).astype(BF16)
            kind = info[0:NVOX, BLOCKS + b : BLOCKS + b + 1]
            goal = jnp.zeros((NVOX, PLANS), F32)
            scale = jnp.zeros((NVOX, PLANS), F32)
            for s in range(NSTRUCT):
                goal = jnp.where(kind == float(s), prescribed[s : s + 1, :], goal)
                scale = jnp.where(kind == float(s), importance[0, s], scale)
            target_dose[b * NVOX : (b + 1) * NVOX, :] = goal
            voxel_weight[b * NVOX : (b + 1) * NVOX, :] = scale

    @pl.loop(0, ITERS)
    def _(it):
        wait(w_buf.at[it], w_rs.at[it])
        high, low = halves(w_buf[it])
        w_cat[:, :PLANS] = high
        w_cat[:, PLANS:] = low
        for c in range(CHUNKS):

            @pl.loop(0, PER * BLK // GROUP)
            def _(g, c=c):
                rows = pl.ds(pl.multiple_of(c * PER * BLK + g * GROUP, GROUP), GROUP)
                part = joined(dot(mat_hi[rows, :], w_cat[...]))
                part = part + dot(mat_lo[rows, :], w_cat[:, :PLANS])
                for k in range(GROUP // BLK):
                    b = g * (GROUP // BLK) + k
                    out_buf[c, pl.ds(b, NDEV, stride=PER), :] = warped(
                        warp[c * PER + b], part[k * BLK : (k + 1) * BLK]
                    )

            send_all(
                lambda to, c=c: out_buf.at[c, pl.ds(to * PER, PER)],
                in_buf.at[it, c, pl.ds(me * PER, PER)],
                out_ss.at[c],
                out_rs.at[it, c],
            )

        @pl.when(it == 0)
        def _():
            tables()

        for c in range(CHUNKS):
            wait(in_buf.at[it, c], out_rs.at[it, c])
            for b in range(PER):
                high, low = halves(in_buf[it, c, pl.ds(b, NDEV, stride=PER), :])
                rows = slice((c * PER + b) * NDEV, (c * PER + b + 1) * NDEV)
                in_cat[rows, :PLANS] = high
                in_cat[rows, PLANS:] = low
            half = slice(c * PER * NDEV, (c + 1) * PER * NDEV)
            part = joined(dot(gather_in[:, half], in_cat[half, :]))
            dose[...] = part if c == 0 else dose[...] + part
        adjoint = voxel_weight[...] * (dose[...] - target_dose[...])
        high, low = halves(adjoint)
        adj_cat[:, :PLANS] = high
        adj_cat[:, PLANS:] = low
        for c in range(CHUNKS):
            for b in range(PER):
                rows = slice((c * PER + b) * NDEV, (c * PER + b + 1) * NDEV)
                back_buf[c, pl.ds(b, NDEV, stride=PER), :] = joined(
                    dot(gather_t[rows, :], adj_cat[...])
                )
            send_all(
                lambda to, c=c: back_buf.at[c, pl.ds(to * PER, PER)],
                adj_buf.at[it, c, pl.ds(me * PER, PER)],
                back_ss.at[c],
                back_rs.at[it, c],
            )

        @pl.when(it == ITERS - 1)
        def _():
            for b in range(BLOCKS):
                field_out[pl.ds(b, NVOX, stride=BLOCKS), :] = dose[b * NVOX : (b + 1) * NVOX, :]
            send_all(
                lambda to: field_out.at[pl.ds(vox_of(to) * BLOCKS, BLOCKS)],
                field_in.at[pl.ds(me * BLOCKS, BLOCKS)],
                field_ss,
                field_rs,
            )

        for c in range(CHUNKS):
            wait(out_buf.at[c, pl.ds(0, (NDEV - 1) * PER)], out_ss.at[c])
        for c in range(CHUNKS):
            wait(adj_buf.at[it, c], back_rs.at[it, c])
            for b in range(PER):
                value = warped(warp_t[c * PER + b], adj_buf[it, c, pl.ds(b, NDEV, stride=PER), :])
                high, low = halves(value)
                rows = slice((c * PER + b) * NDEV, (c * PER + b + 1) * NDEV)
                la_cat[rows, :PLANS] = high
                la_cat[rows, PLANS:] = low

        @pl.loop(0, SPOTS // GROUP)
        def _(g):
            rows = pl.ds(pl.multiple_of(g * GROUP, GROUP), GROUP)
            part = joined(dot(tra_hi[rows, :], la_cat[...]))
            grad[rows, :] = part + dot(tra_lo[rows, :], la_cat[:, :PLANS])

        send_all(
            lambda to: grad.at[pl.ds(to * OWN, OWN)],
            grad_in.at[it, pl.ds(me * OWN, OWN)],
            grad_ss,
            grad_rs.at[it],
        )
        for c in range(CHUNKS):
            wait(back_buf.at[c, pl.ds(0, (NDEV - 1) * PER)], back_ss.at[c])
        wait(grad_in.at[it], grad_rs.at[it])
        for r in range(OWN):
            total = jnp.sum(grad_in[it, pl.ds(r, NDEV, stride=OWN), :], axis=0, keepdims=True)
            w_next[r : r + 1, :] = jnp.maximum(w_own[r : r + 1, :] - step[...] * total, 0.0)
        w_own[...] = w_next[0:OWN, :]

        @pl.when(it < ITERS - 1)
        def _():
            send_all(
                lambda to: w_next.at[pl.ds(0, OWN)],
                w_buf.at[it + 1, pl.ds(me * OWN, OWN)],
                w_ss.at[it + 1],
                w_rs.at[it + 1],
            )
            wait(w_buf.at[it, pl.ds(0, (NDEV - 1) * OWN)], w_ss.at[it + 1])

        wait(grad.at[pl.ds(0, (NDEV - 1) * OWN)], grad_ss)

    new_weights[...] = w_own[...]
    wait(w_buf.at[0, pl.ds(0, (NDEV - 1) * OWN)], w_ss.at[0])
    wait(info_in.at[pl.ds(0, NDEV - 1)], info_ss)
    wait(field_in, field_rs)
    for b in range(BLOCKS):
        dose_out[b * BLK : (b + 1) * BLK, :] = field_in[pl.ds(b, NDEV, stride=BLOCKS), :]
    wait(field_in.at[pl.ds(0, (NDEV - 1) * BLOCKS)], field_ss)


def per_device(
    influence,
    weights,
    warp_tiles,
    owners,
    owner_slot,
    tile_index,
    structure,
    prescribed,
    importance,
    step_size,
):
    vmem = pl.BlockSpec(memory_space=pltpu.VMEM)
    smem = pl.BlockSpec(memory_space=pltpu.SMEM)
    hbm = pl.BlockSpec(memory_space=pl.ANY)
    dma = pltpu.SemaphoreType.DMA
    scratch = [
        pltpu.VMEM((4, LOAD, SPOTS), F32),
        pltpu.VMEM((ROWS, SPOTS), BF16),
        pltpu.VMEM((ROWS, SPOTS), BF16),
        pltpu.VMEM((SPOTS, ROWS), BF16),
        pltpu.VMEM((SPOTS, ROWS), BF16),
        pltpu.VMEM((NTILE, BLK, BLK), F32),
        pltpu.VMEM((BLOCKS, BLK, 3 * BLK), BF16),
        pltpu.VMEM((BLOCKS, BLK, 3 * BLK), BF16),
        pltpu.VMEM((BLK, BLK), F32),
        pltpu.VMEM((BLK, BLK), F32),
        pltpu.VMEM((TARGETS, SOURCES), BF16),
        pltpu.VMEM((SOURCES, TARGETS), BF16),
        pltpu.VMEM((ITERS, SPOTS, PLANS), F32),
        pltpu.VMEM((SPOTS, 2 * PLANS), BF16),
        pltpu.VMEM((OWN, PLANS), F32),
        pltpu.VMEM((16, PLANS), F32),
        pltpu.VMEM((CHUNKS, NDEV * PER, PLANS), F32),
        pltpu.VMEM((ITERS, CHUNKS, NDEV * PER, PLANS), F32),
        pltpu.VMEM((SOURCES, 2 * PLANS), BF16),
        pltpu.VMEM((TARGETS, PLANS), F32),
        pltpu.VMEM((TARGETS, PLANS), F32),
        pltpu.VMEM((TARGETS, PLANS), F32),
        pltpu.VMEM((TARGETS, 2 * PLANS), BF16),
        pltpu.VMEM((CHUNKS, NDEV * PER, PLANS), F32),
        pltpu.VMEM((ITERS, CHUNKS, NDEV * PER, PLANS), F32),
        pltpu.VMEM((ROWS, 2 * PLANS), BF16),
        pltpu.VMEM((SPOTS, PLANS), F32),
        pltpu.VMEM((ITERS, SPOTS, PLANS), F32),
        pltpu.VMEM((NVOX * BLOCKS, PLANS), F32),
        pltpu.VMEM((NDEV * BLOCKS, PLANS), F32),
        dma((4,)),
        dma,
        dma,
        dma,
        dma((ITERS,)),
        dma((ITERS,)),
        dma((CHUNKS,)),
        dma((ITERS, CHUNKS)),
        dma((CHUNKS,)),
        dma((ITERS, CHUNKS)),
        dma,
        dma((ITERS,)),
        dma,
        dma,
    ]
    return pl.pallas_call(
        kernel,
        out_shape=(
            jax.ShapeDtypeStruct((OWN, PLANS), F32),
            jax.ShapeDtypeStruct((ROWS, PLANS), F32),
        ),
        in_specs=[smem, smem, hbm, vmem, hbm, vmem, vmem, vmem, vmem, vmem],
        out_specs=(vmem, vmem),
        scratch_shapes=scratch,
        compiler_params=pltpu.CompilerParams(
            collective_id=0, has_side_effects=True, vmem_limit_bytes=67043328
        ),
    )(
        tile_index,
        importance.reshape(1, NSTRUCT),
        influence,
        weights,
        warp_tiles,
        owners.reshape(1, BLOCKS),
        owner_slot,
        structure.reshape(BLOCKS, BLK),
        prescribed,
        step_size.reshape(1, PLANS),
    )


def solution(mesh):
    split = Mesh(mesh.devices.reshape(SIZES), AXES)
    both = P("z", VOX)
    placed = (
        P("z", VOX, None),
        P(AXES, None),
        P(),
        P("z", VOX, None),
        both,
        both,
        P(VOX),
        P(),
        P(),
        P(),
    )
    return jax.shard_map(
        per_device,
        mesh=split,
        in_specs=placed,
        out_specs=(P(AXES, None), P(VOX, None)),
        check_vma=False,
    )
```

```python
import jax
import jax.numpy as jnp
from jax import lax
from jax.experimental import pallas as pl
from jax.experimental.pallas import tpu as pltpu
from jax.sharding import Mesh
from jax.sharding import PartitionSpec as P

AXES = ("z", "x", "y", "c")
VOX = ("x", "y", "c")
SIZES = (4, 4, 4, 2)
NDEV = 128
NVOX = 32
NSTRUCT = 8
ITERS = 2
PLANS = 128
BLK = 128
BLOCKS = 16
CHUNKS = 2
PER = BLOCKS // CHUNKS
SPOTS = 1536
OWN = SPOTS // NDEV
ROWS = BLOCKS * BLK
TARGETS = NVOX * BLOCKS
SOURCES = NDEV * BLOCKS
NTILE = 64
LOAD = 256
GROUP = 512
LAYER = SPOTS // 4
LOGICAL = pl.DeviceIdType.LOGICAL
F32 = jnp.float32
BF16 = jnp.bfloat16


def offset_parts(offset):
    return offset // 32, (offset // 8) % 4, (offset // 2) % 4, offset % 2


def hops(offset):
    z, x, y, c = offset_parts(offset)
    return 2 * (min(z, 4 - z) + min(x, 4 - x) + min(y, 4 - y)) + c


OFFSETS = sorted(range(1, NDEV), key=lambda o: -hops(o))


def peers():
    z, x, y, c = [lax.axis_index(a) for a in AXES]
    pz = [lax.rem(z + d, 4) * 32 for d in range(4)]
    px = [lax.rem(x + d, 4) * 8 for d in range(4)]
    py = [lax.rem(y + d, 4) * 2 for d in range(4)]
    pc = [lax.rem(c + d, 2) for d in range(2)]
    zx = [[pz[a] + px[b] for b in range(4)] for a in range(4)]
    yc = [[py[a] + pc[b] for b in range(2)] for a in range(4)]

    def index(offset):
        dz, dx, dy, dc = offset_parts(offset)
        return zx[dz][dx] + yc[dy][dc]

    return index


def halves(value):
    high = value.astype(BF16)
    low = (value - high.astype(F32)).astype(BF16)
    return high, low


def dot(a, b):
    return jnp.dot(a, b, preferred_element_type=F32)


def joined(pair):
    return pair[:, :PLANS] + pair[:, PLANS:]


def kernel(
    tile_ids,
    importance,
    influence,
    weights,
    tiles,
    owners,
    slots,
    structure,
    prescribed,
    step,
    new_weights,
    dose_out,
    staged,
    mat_hi,
    mat_lo,
    tra_hi,
    tra_lo,
    tile_buf,
    warp,
    warp_t,
    info_out,
    info_in,
    gather_in,
    gather_t,
    w_buf,
    w_cat,
    w_own,
    w_next,
    out_buf,
    in_buf,
    in_cat,
    dose,
    target_dose,
    voxel_weight,
    adj_cat,
    back_buf,
    adj_buf,
    la_cat,
    grad,
    grad_in,
    field_out,
    field_in,
    load_sem,
    tile_sem,
    info_ss,
    info_rs,
    w_ss,
    w_rs,
    out_ss,
    out_rs,
    back_ss,
    back_rs,
    grad_ss,
    grad_rs,
    field_ss,
    field_rs,
):
    index = peers()
    me = index(0)
    vox_of = lambda device: lax.rem(device, NVOX)

    def send(src, dst, send_sem, recv_sem, to):
        pltpu.make_async_remote_copy(
            src_ref=src,
            dst_ref=dst,
            send_sem=send_sem,
            recv_sem=recv_sem,
            device_id=to,
            device_id_type=LOGICAL,
        ).start()

    def send_all(src, dst, send_sem, recv_sem):
        for o in OFFSETS:
            send(src(index(o)), dst, send_sem, recv_sem, index(o))
        pltpu.make_async_copy(src(me), dst, recv_sem).start()

    def wait(ref, sem):
        pltpu.make_async_copy(ref, ref, sem).wait()

    stored = pltpu.make_async_copy(field_in, dose_out, tile_sem)
    loads = []
    for n in range(ROWS // LOAD):
        loads.append(
            pltpu.make_async_copy(
                influence.at[0, pl.ds(n * LOAD, LOAD)], staged.at[n % 4], load_sem.at[n % 4]
            )
        )
    for n in range(4):
        loads[n].start()
    tile_load = pltpu.make_async_copy(tiles, tile_buf, tile_sem)
    tile_load.start()

    barrier = pltpu.get_barrier_semaphore()
    for o in OFFSETS:
        pl.semaphore_signal(barrier, inc=1, device_id=index(o), device_id_type=LOGICAL)

    info_out[...] = jnp.zeros((BLK, BLK), F32)
    info_out[BLOCKS : 2 * BLOCKS, :] = structure[...].astype(F32)
    turned = info_out[...].T
    w_next[0:1, 0:BLOCKS] = (slots[...] * NVOX + owners[...]).astype(F32)
    lane = lax.broadcasted_iota(jnp.int32, (BLK, BLK), 1)
    info_out[...] = jnp.where(lane < BLOCKS, w_next[0:1, :], turned)

    for n in range(ROWS // LOAD):
        loads[n].wait()

        @pl.loop(0, SPOTS // BLK)
        def _(k, n=n):
            cols = pl.ds(pl.multiple_of(k * BLK, BLK), BLK)
            rows = pl.ds(n * LOAD, LOAD)
            high, low = halves(staged[n % 4, :, cols])
            mat_hi[rows, cols] = high
            mat_lo[rows, cols] = low

        if n + 4 < ROWS // LOAD:
            loads[n + 4].start()

    tile_load.wait()

    @pl.loop(0, BLOCKS)
    def _(b):
        tile = tile_buf[tile_ids[0, b]]
        high, low = halves(tile)
        warp[b, :, 0:BLK] = high
        warp[b, :, BLK : 2 * BLK] = low
        warp[b, :, 2 * BLK :] = high
        high, low = halves(tile.T)
        warp_t[b, :, 0:BLK] = high
        warp_t[b, :, BLK : 2 * BLK] = low
        warp_t[b, :, 2 * BLK :] = high

    w_own[...] = weights[...]
    pl.semaphore_wait(barrier, NDEV - 1)
    send_all(lambda to: weights, w_buf.at[0, pl.ds(me * OWN, OWN)], w_ss.at[0], w_rs.at[0])
    send_all(
        lambda to: info_out.at[pl.ds(to, 1)], info_in.at[pl.ds(me, 1)], info_ss, info_rs
    )

    @pl.loop(0, SPOTS // BLK)
    def _(k):
        cols = pl.ds(pl.multiple_of(k * BLK, BLK), BLK)
        for n in range(ROWS // GROUP):
            rows = slice(n * GROUP, (n + 1) * GROUP)
            tra_hi[cols, rows] = mat_hi[rows, cols].T
            tra_lo[cols, rows] = mat_lo[rows, cols].T

    def warped(matrix, value):
        high, low = halves(value)
        return dot(matrix, jnp.concatenate([high, high, low], axis=0))

    def tables():
        wait(info_in, info_rs)
        info = info_in[...]
        turned = info.T
        down = lax.broadcasted_iota(jnp.int32, (TARGETS, BLK), 0).astype(F32)
        across = lax.broadcasted_iota(jnp.int32, (BLK, TARGETS), 1).astype(F32)
        for b in range(BLOCKS):
            at = slice(b * BLK, (b + 1) * BLK)
            gather_in[:, at] = jnp.where(down == turned[b : b + 1, :], 1.0, 0.0).astype(BF16)
            gather_t[at, :] = jnp.where(across == info[:, b : b + 1], 1.0, 0.0).astype(BF16)
            kind = info[0:NVOX, BLOCKS + b : BLOCKS + b + 1]
            goal = jnp.zeros((NVOX, PLANS), F32)
            scale = jnp.zeros((NVOX, PLANS), F32)
            for s in range(NSTRUCT):
                goal = jnp.where(kind == float(s), prescribed[s : s + 1, :], goal)
                scale = jnp.where(kind == float(s), importance[0, s], scale)
            target_dose[b * NVOX : (b + 1) * NVOX, :] = goal
            voxel_weight[b * NVOX : (b + 1) * NVOX, :] = scale

    @pl.loop(0, ITERS)
    def _(it):
        wait(w_buf.at[it], w_rs.at[it])
        high, low = halves(w_buf[it])
        w_cat[:, :PLANS] = high
        w_cat[:, PLANS:] = low
        for c in range(CHUNKS):

            @pl.loop(0, PER * BLK // GROUP)
            def _(g, c=c):
                rows = pl.ds(pl.multiple_of(c * PER * BLK + g * GROUP, GROUP), GROUP)
                part = joined(dot(mat_hi[rows, :], w_cat[...]))
                part = part + dot(mat_lo[rows, :], w_cat[:, :PLANS])
                for k in range(GROUP // BLK):
                    b = g * (GROUP // BLK) + k
                    out_buf[c, pl.ds(b, NDEV, stride=PER), :] = warped(
                        warp[c * PER + b], part[k * BLK : (k + 1) * BLK]
                    )

            send_all(
                lambda to, c=c: out_buf.at[c, pl.ds(to * PER, PER)],
                in_buf.at[it, c, pl.ds(me * PER, PER)],
                out_ss.at[c],
                out_rs.at[it, c],
            )

        @pl.when(it == 0)
        def _():
            tables()

        for c in range(CHUNKS):
            wait(in_buf.at[it, c], out_rs.at[it, c])
            for b in range(PER):
                high, low = halves(in_buf[it, c, pl.ds(b, NDEV, stride=PER), :])
                rows = slice((c * PER + b) * NDEV, (c * PER + b + 1) * NDEV)
                in_cat[rows, :PLANS] = high
                in_cat[rows, PLANS:] = low
            half = slice(c * PER * NDEV, (c + 1) * PER * NDEV)
            part = joined(dot(gather_in[:, half], in_cat[half, :]))
            dose[...] = part if c == 0 else dose[...] + part
        adjoint = voxel_weight[...] * (dose[...] - target_dose[...])
        high, low = halves(adjoint)
        adj_cat[:, :PLANS] = high
        adj_cat[:, PLANS:] = low
        for c in range(CHUNKS):
            for b in range(PER):
                rows = slice((c * PER + b) * NDEV, (c * PER + b + 1) * NDEV)
                back_buf[c, pl.ds(b, NDEV, stride=PER), :] = joined(
                    dot(gather_t[rows, :], adj_cat[...])
                )
            send_all(
                lambda to, c=c: back_buf.at[c, pl.ds(to * PER, PER)],
                adj_buf.at[it, c, pl.ds(me * PER, PER)],
                back_ss.at[c],
                back_rs.at[it, c],
            )

        @pl.when(it == ITERS - 1)
        def _():
            for b in range(BLOCKS):
                field_out[pl.ds(b, NVOX, stride=BLOCKS), :] = dose[b * NVOX : (b + 1) * NVOX, :]
            send_all(
                lambda to: field_out.at[pl.ds(vox_of(to) * BLOCKS, BLOCKS)],
                field_in.at[pl.ds(me * BLOCKS, BLOCKS)],
                field_ss,
                field_rs,
            )

        for c in range(CHUNKS):
            wait(out_buf.at[c, pl.ds(0, (NDEV - 1) * PER)], out_ss.at[c])
        def spread(c):
            wait(adj_buf.at[it, c], back_rs.at[it, c])
            for b in range(PER):
                value = warped(warp_t[c * PER + b], adj_buf[it, c, pl.ds(b, NDEV, stride=PER), :])
                high, low = halves(value)
                rows = slice((c * PER + b) * NDEV, (c * PER + b + 1) * NDEV)
                la_cat[rows, :PLANS] = high
                la_cat[rows, PLANS:] = low

        def pulled(rows, c):
            half = slice(c * PER * NDEV, (c + 1) * PER * NDEV)
            part = joined(dot(tra_hi[rows, half], la_cat[half, :]))
            return part + dot(tra_lo[rows, half], la_cat[half, :PLANS])

        spread(0)

        @pl.loop(0, SPOTS // LAYER)
        def _(g):
            rows = pl.ds(pl.multiple_of(g * LAYER, LAYER), LAYER)
            grad[rows, :] = pulled(rows, 0)

        spread(1)
        own = grad_in.at[it, pl.ds(me * OWN, OWN)]
        for dz in (2, 1, 3, 0):
            first = index(dz * 32) // 32 * LAYER
            rows = pl.ds(pl.multiple_of(first, LAYER), LAYER)
            grad[rows, :] = grad[rows, :] + pulled(rows, 1)
            for o in OFFSETS:
                if o // 32 == dz:
                    send(grad.at[pl.ds(index(o) * OWN, OWN)], own, grad_ss, grad_rs.at[it], index(o))
        pltpu.make_async_copy(grad.at[pl.ds(me * OWN, OWN)], own, grad_rs.at[it]).start()
        for c in range(CHUNKS):
            wait(back_buf.at[c, pl.ds(0, (NDEV - 1) * PER)], back_ss.at[c])

        @pl.when(it == ITERS - 1)
        def _():
            wait(field_in, field_rs)
            stored.start()

        wait(grad_in.at[it], grad_rs.at[it])
        for r in range(OWN):
            total = jnp.sum(grad_in[it, pl.ds(r, NDEV, stride=OWN), :], axis=0, keepdims=True)
            w_next[r : r + 1, :] = jnp.maximum(w_own[r : r + 1, :] - step[...] * total, 0.0)
        w_own[...] = w_next[0:OWN, :]

        @pl.when(it < ITERS - 1)
        def _():
            send_all(
                lambda to: w_next.at[pl.ds(0, OWN)],
                w_buf.at[it + 1, pl.ds(me * OWN, OWN)],
                w_ss.at[it + 1],
                w_rs.at[it + 1],
            )
            wait(w_buf.at[it, pl.ds(0, (NDEV - 1) * OWN)], w_ss.at[it + 1])

        wait(grad.at[pl.ds(0, (NDEV - 1) * OWN)], grad_ss)

    new_weights[...] = w_own[...]
    wait(w_buf.at[0, pl.ds(0, (NDEV - 1) * OWN)], w_ss.at[0])
    wait(info_in.at[pl.ds(0, NDEV - 1)], info_ss)
    wait(field_in.at[pl.ds(0, (NDEV - 1) * BLOCKS)], field_ss)
    stored.wait()


def finish(weights, field, new_weights, dose_field):
    new_weights[...] = weights[...]
    for b in range(BLOCKS):
        dose_field[b * BLK : (b + 1) * BLK, :] = field[pl.ds(b, NDEV, stride=BLOCKS), :]


def per_device(
    influence,
    weights,
    warp_tiles,
    owners,
    owner_slot,
    tile_index,
    structure,
    prescribed,
    importance,
    step_size,
):
    vmem = pl.BlockSpec(memory_space=pltpu.VMEM)
    smem = pl.BlockSpec(memory_space=pltpu.SMEM)
    hbm = pl.BlockSpec(memory_space=pl.ANY)
    dma = pltpu.SemaphoreType.DMA
    scratch = [
        pltpu.VMEM((4, LOAD, SPOTS), F32),
        pltpu.VMEM((ROWS, SPOTS), BF16),
        pltpu.VMEM((ROWS, SPOTS), BF16),
        pltpu.VMEM((SPOTS, ROWS), BF16),
        pltpu.VMEM((SPOTS, ROWS), BF16),
        pltpu.VMEM((NTILE, BLK, BLK), F32),
        pltpu.VMEM((BLOCKS, BLK, 3 * BLK), BF16),
        pltpu.VMEM((BLOCKS, BLK, 3 * BLK), BF16),
        pltpu.VMEM((BLK, BLK), F32),
        pltpu.VMEM((BLK, BLK), F32),
        pltpu.VMEM((TARGETS, SOURCES), BF16),
        pltpu.VMEM((SOURCES, TARGETS), BF16),
        pltpu.VMEM((ITERS, SPOTS, PLANS), F32),
        pltpu.VMEM((SPOTS, 2 * PLANS), BF16),
        pltpu.VMEM((OWN, PLANS), F32),
        pltpu.VMEM((16, PLANS), F32),
        pltpu.VMEM((CHUNKS, NDEV * PER, PLANS), F32),
        pltpu.VMEM((ITERS, CHUNKS, NDEV * PER, PLANS), F32),
        pltpu.VMEM((SOURCES, 2 * PLANS), BF16),
        pltpu.VMEM((TARGETS, PLANS), F32),
        pltpu.VMEM((TARGETS, PLANS), F32),
        pltpu.VMEM((TARGETS, PLANS), F32),
        pltpu.VMEM((TARGETS, 2 * PLANS), BF16),
        pltpu.VMEM((CHUNKS, NDEV * PER, PLANS), F32),
        pltpu.VMEM((ITERS, CHUNKS, NDEV * PER, PLANS), F32),
        pltpu.VMEM((ROWS, 2 * PLANS), BF16),
        pltpu.VMEM((SPOTS, PLANS), F32),
        pltpu.VMEM((ITERS, SPOTS, PLANS), F32),
        pltpu.VMEM((NVOX * BLOCKS, PLANS), F32),
        pltpu.VMEM((NDEV * BLOCKS, PLANS), F32),
        dma((4,)),
        dma,
        dma,
        dma,
        dma((ITERS,)),
        dma((ITERS,)),
        dma((CHUNKS,)),
        dma((ITERS, CHUNKS)),
        dma((CHUNKS,)),
        dma((ITERS, CHUNKS)),
        dma,
        dma((ITERS,)),
        dma,
        dma,
    ]
    outs = (
        jax.ShapeDtypeStruct((OWN, PLANS), F32),
        jax.ShapeDtypeStruct((ROWS, PLANS), F32),
    )
    final_weights, field = pl.pallas_call(
        kernel,
        out_shape=outs,
        in_specs=[smem, smem, hbm, vmem, hbm, vmem, vmem, vmem, vmem, vmem],
        out_specs=(vmem, hbm),
        scratch_shapes=scratch,
        compiler_params=pltpu.CompilerParams(
            collective_id=0, has_side_effects=True, vmem_limit_bytes=67043328
        ),
    )(
        tile_index,
        importance.reshape(1, NSTRUCT),
        influence,
        weights,
        warp_tiles,
        owners.reshape(1, BLOCKS),
        owner_slot,
        structure.reshape(BLOCKS, BLK),
        prescribed,
        step_size.reshape(1, PLANS),
    )
    return pl.pallas_call(
        finish, out_shape=outs, in_specs=[vmem, vmem], out_specs=(vmem, vmem)
    )(final_weights, field)


def solution(mesh):
    split = Mesh(mesh.devices.reshape(SIZES), AXES)
    both = P("z", VOX)
    placed = (
        P("z", VOX, None),
        P(AXES, None),
        P(),
        P("z", VOX, None),
        both,
        both,
        P(VOX),
        P(),
        P(),
        P(),
    )
    return jax.shard_map(
        per_device,
        mesh=split,
        in_specs=placed,
        out_specs=(P(AXES, None), P(VOX, None)),
        check_vma=False,
    )
```

```python
import jax
import jax.numpy as jnp
from jax import lax
from jax.experimental import pallas as pl
from jax.experimental.pallas import tpu as pltpu
from jax.sharding import Mesh
from jax.sharding import PartitionSpec as P

AXES = ("z", "x", "y", "c")
VOX = ("x", "y", "c")
SIZES = (4, 4, 4, 2)
NDEV = 128
NVOX = 32
NSTRUCT = 8
ITERS = 2
PLANS = 128
BLK = 128
BLOCKS = 16
PARTS = 2
PER = BLOCKS // PARTS
SPOTS = 1536
OWN = SPOTS // NDEV
PACKED = OWN // PARTS
ROWS = BLOCKS * BLK
TARGETS = NVOX * BLOCKS
SOURCES = NDEV * BLOCKS
NTILE = 64
LOAD = 256
LOADS = ROWS // LOAD
GROUP = 512
DEPOSIT = 0
LATE = 2
EARLY = 3
PAIR = GROUP // 2
LAYER = SPOTS // 4
LOGICAL = pl.DeviceIdType.LOGICAL
F32 = jnp.float32
BF16 = jnp.bfloat16


def offset_parts(offset):
    return offset // 32, (offset // 8) % 4, (offset // 2) % 4, offset % 2


def hops(offset):
    z, x, y, c = offset_parts(offset)
    return 2 * (min(z, 4 - z) + min(x, 4 - x) + min(y, 4 - y)) + c


OFFSETS = sorted(range(1, NDEV), key=lambda o: -hops(o))
CHIPS = [o for o in OFFSETS if o % 2 == 0]
NCHIP = NDEV // 2


def peers():
    z, x, y, c = [lax.axis_index(a) for a in AXES]
    pz = [lax.rem(z + d, 4) * 32 for d in range(4)]
    px = [lax.rem(x + d, 4) * 8 for d in range(4)]
    py = [lax.rem(y + d, 4) * 2 for d in range(4)]
    pc = [lax.rem(c + d, 2) for d in range(2)]
    zx = [[pz[a] + px[b] for b in range(4)] for a in range(4)]
    yc = [[py[a] + pc[b] for b in range(2)] for a in range(4)]

    def index(offset):
        dz, dx, dy, dc = offset_parts(offset)
        return zx[dz][dx] + yc[dy][dc]

    return index


def halves(value):
    high = value.astype(BF16)
    low = (value - high.astype(F32)).astype(BF16)
    return high, low


def dot(a, b):
    return jnp.dot(a, b, preferred_element_type=F32)


def left(rows):
    return lax.broadcasted_iota(jnp.int32, (rows, PLANS), 1) < PLANS // 2


def swapped(value):
    return pltpu.roll(value, PLANS // 2, 1)


def joined(pair):
    return pair[:, :PLANS] + pair[:, PLANS:]


def kernel(
    tile_ids,
    importance,
    influence,
    weights,
    tiles,
    owners,
    slots,
    structure,
    prescribed,
    step,
    new_weights,
    dose_out,
    staged,
    mat_hi,
    mat_lo,
    tra_hi,
    tra_lo,
    tile_buf,
    warp,
    warp_t,
    info_out,
    info_in,
    gather_in,
    gather_t,
    w_buf,
    w_flat,
    w_cat,
    w_own,
    step_buf,
    out_buf,
    in_buf,
    in_cat,
    dose,
    target_dose,
    voxel_weight,
    adj_cat,
    back_buf,
    adj_buf,
    la_cat,
    flat,
    grad,
    pair_in,
    grad_sum,
    grad_in,
    field_out,
    field_in,
    field,
    load_sem,
    tile_sem,
    info_ss,
    info_rs,
    w_ss,
    w_rs,
    pass_ss,
    pass_rs,
    out_ss,
    out_rs,
    back_ss,
    back_rs,
    pair_ss,
    pair_rs,
    grad_ss,
    grad_rs,
    field_ss,
    field_rs,
):
    index = peers()
    me = index(0)
    partner = index(1)
    chip = me // 2
    vox_of = lambda device: lax.rem(device, NVOX)

    def send(src, dst, send_sem, recv_sem, to):
        pltpu.make_async_remote_copy(
            src_ref=src,
            dst_ref=dst,
            send_sem=send_sem,
            recv_sem=recv_sem,
            device_id=to,
            device_id_type=LOGICAL,
        ).start()

    def send_all(src, dst, send_sem, recv_sem):
        for o in OFFSETS:
            send(src(index(o)), dst, send_sem, recv_sem, index(o))
        pltpu.make_async_copy(src(me), dst, recv_sem).start()

    def wait(ref, sem):
        pltpu.make_async_copy(ref, ref, sem).wait()

    stored = pltpu.make_async_copy(field, dose_out, tile_sem)
    loads = []
    for n in range(LOADS):
        loads.append(
            pltpu.make_async_copy(
                influence.at[0, pl.ds(n * LOAD, LOAD)], staged.at[n % 4], load_sem.at[n % 4]
            )
        )
    for n in range(4):
        loads[n].start()
    tile_load = pltpu.make_async_copy(tiles, tile_buf, tile_sem)
    tile_load.start()

    barrier = pltpu.get_barrier_semaphore()
    for o in OFFSETS:
        pl.semaphore_signal(barrier, inc=1, device_id=index(o), device_id_type=LOGICAL)

    info_out[...] = jnp.zeros((BLK, BLK), F32)
    info_out[BLOCKS : 2 * BLOCKS, :] = structure[...].astype(F32)
    turned = info_out[...].T
    flat[0:1, 0:BLOCKS] = (slots[...] * NVOX + owners[...]).astype(F32)
    lane = lax.broadcasted_iota(jnp.int32, (BLK, BLK), 1)
    info_out[...] = jnp.where(lane < BLOCKS, flat[0:1, :], turned)

    def place(b):
        return 2 * (b % PER) + b // PER

    def convert(n):
        loads[n].wait()

        @pl.loop(0, SPOTS // BLK)
        def _(k):
            cols = pl.ds(pl.multiple_of(k * BLK, BLK), BLK)
            for h in range(LOAD // BLK):
                high, low = halves(staged[n % 4, h * BLK : (h + 1) * BLK, cols])
                rows = pl.ds(place(n * (LOAD // BLK) + h) * BLK, BLK)
                mat_hi[rows, cols] = high
                mat_lo[rows, cols] = low

        if n + 4 < LOADS:
            loads[n + 4].start()

    for n in range(EARLY):
        convert(n)

    even = weights[pl.ds(0, PACKED, stride=2), :]
    odd = weights[pl.ds(1, PACKED, stride=2), :]
    w_own[0, 0, 0:PACKED, :] = jnp.where(left(PACKED), even, swapped(odd))
    w_own[0, 1, 0:PACKED, :] = jnp.where(left(PACKED), swapped(even), odd)
    step_buf[0:1, :] = jnp.where(left(1), step[...], swapped(step[...]))
    step_buf[1:2, :] = jnp.where(left(1), swapped(step[...]), step[...])
    pl.semaphore_wait(barrier, NDEV - 1)

    def share(it, h):
        source = w_own.at[it, h, pl.ds(0, PACKED)]
        own = w_buf.at[it, h, pl.ds(me * PACKED, PACKED)]
        for o in CHIPS:
            send(source, own, w_ss.at[it, h], w_rs.at[it, h], index(o))
        pltpu.make_async_copy(source, own, w_rs.at[it, h]).start()

    def forward(it, h):
        wait(w_buf.at[it, h, pl.ds(0, NCHIP * PACKED)], w_rs.at[it, h])
        for k in range(NCHIP):
            rows = w_buf.at[it, h, pl.ds((2 * k + me % 2) * PACKED, PACKED)]
            send(rows, rows, pass_ss.at[it, h], pass_rs.at[it, h], partner)

    send_all(
        lambda to: info_out.at[pl.ds(to, 1)], info_in.at[pl.ds(me, 1)], info_ss, info_rs
    )
    share(0, 0)
    share(0, 1)
    for n in range(EARLY, LOADS):
        convert(n)
    tile_load.wait()

    @pl.loop(0, BLOCKS)
    def _(b):
        tile = tile_buf[tile_ids[0, b]]
        high, low = halves(tile)
        warp[b, :, 0:BLK] = high
        warp[b, :, BLK : 2 * BLK] = low
        warp[b, :, 2 * BLK :] = high
        high, low = halves(tile.T)
        warp_t[b, :, 0:BLK] = high
        warp_t[b, :, BLK : 2 * BLK] = low
        warp_t[b, :, 2 * BLK :] = high

    def turn(h):
        @pl.loop(0, SPOTS // BLK // PARTS)
        def _(k):
            cols = pl.ds(pl.multiple_of(h * (SPOTS // PARTS) + k * BLK, BLK), BLK)
            for n in range(ROWS // GROUP):
                rows = slice(n * GROUP, (n + 1) * GROUP)
                tra_hi[cols, rows] = mat_hi[rows, cols].T
                tra_lo[cols, rows] = mat_lo[rows, cols].T

    def warped(matrix, value):
        high, low = halves(value)
        return dot(matrix, jnp.concatenate([high, high, low], axis=0))

    def tables():
        wait(info_in, info_rs)
        info = info_in[...]
        turned = info.T
        down = lax.broadcasted_iota(jnp.int32, (BLK, BLK), 0).astype(F32)
        across = lax.broadcasted_iota(jnp.int32, (1, BLK), 1).astype(F32)
        for b in range(BLOCKS):
            at = slice(b * BLK, (b + 1) * BLK)
            row, column = turned[b : b + 1, :], info[:, b : b + 1]
            for n in range(TARGETS // BLK):
                to = slice(n * BLK, (n + 1) * BLK)
                hit = down == row - float(n * BLK)
                gather_in[to, at] = jnp.where(hit, 1.0, 0.0).astype(BF16)
                hit = column == across + float(n * BLK)
                gather_t[at, to] = jnp.where(hit, 1.0, 0.0).astype(BF16)
            kind = info[0:NVOX, BLOCKS + b : BLOCKS + b + 1]
            goal = jnp.zeros((NVOX, PLANS), F32)
            scale = jnp.zeros((NVOX, PLANS), F32)
            for s in range(NSTRUCT):
                goal = jnp.where(kind == float(s), prescribed[s : s + 1, :], goal)
                scale = jnp.where(kind == float(s), importance[0, s], scale)
            at = slice(b * NVOX, (b + 1) * NVOX)
            target_dose[0, at, :] = jnp.where(left(NVOX), goal, swapped(goal))
            target_dose[1, at, :] = jnp.where(left(NVOX), swapped(goal), goal)
            voxel_weight[at, :] = scale

    forward(0, 0)
    tables()

    @pl.loop(0, ITERS)
    def _(it):
        @pl.loop(0, PARTS)
        def _(h):
            pl.when((it > 0) & (h == 0))(lambda: forward(it, h))
            wait(w_buf.at[it, h, pl.ds(0, NCHIP * PACKED)], pass_rs.at[it, h])
            pair = w_buf[it, h]
            turned = swapped(pair)
            near = left(SPOTS // 2)
            w_flat[pl.ds(0, SPOTS // 2, stride=2), :] = jnp.where(near, pair, turned)
            w_flat[pl.ds(1, SPOTS // 2, stride=2), :] = jnp.where(near, turned, pair)
            high, low = halves(w_flat[...])
            w_cat[:, :PLANS] = high
            w_cat[:, PLANS:] = low

            @pl.loop(0, ROWS // GROUP)
            def _(g):
                pl.when((g == LATE) & (h == 0))(lambda: forward(it, 1))
                rows = pl.ds(pl.multiple_of(g * GROUP, GROUP), GROUP)
                part = joined(dot(mat_hi[rows, :], w_cat[...]))
                part = part + dot(mat_lo[rows, :], w_cat[:, :PLANS])
                for k in range(PAIR // BLK):
                    b = g * (PAIR // BLK) + k
                    at = 2 * k * BLK
                    first = warped(warp[b], part[at : at + BLK])
                    second = warped(warp[PER + b], part[at + BLK : at + 2 * BLK])
                    out_buf[h, pl.ds(b, NDEV, stride=PER), :] = jnp.where(left(BLK), first, second)

            send_all(
                lambda to: out_buf.at[h, pl.ds(to * PER, PER)],
                in_buf.at[it, h, pl.ds(me * PER, PER)],
                out_ss.at[h],
                out_rs.at[it, h],
            )

        @pl.loop(0, PARTS)
        def _(h):
            pl.when(it == 0)(lambda: turn(h))
            wait(in_buf.at[it, h], out_rs.at[it, h])
            for b in range(PER):
                high, low = halves(in_buf[it, h, pl.ds(b, NDEV, stride=PER), :])
                in_cat[b * NDEV : (b + 1) * NDEV, :PLANS] = high
                in_cat[b * NDEV : (b + 1) * NDEV, PLANS:] = low
            near = left(TARGETS)
            total = jnp.where(
                near,
                joined(dot(gather_in[:, : PER * NDEV], in_cat[...])),
                joined(dot(gather_in[:, PER * NDEV :], in_cat[...])),
            )
            total = total + swapped(total)
            dose[h] = total
            high, low = halves(voxel_weight[...] * (total - target_dose[h]))
            adj_cat[:, :PLANS] = high
            adj_cat[:, PLANS:] = low
            for b in range(0, PER, PAIR // BLK):
                first = joined(dot(gather_t[b * NDEV : b * NDEV + PAIR, :], adj_cat[...]))
                second = (PER + b) * NDEV
                second = joined(dot(gather_t[second : second + PAIR, :], adj_cat[...]))
                both = jnp.where(left(PAIR), first, second)
                for k in range(PAIR // BLK):
                    back_buf[h, pl.ds(b + k, NDEV, stride=PER), :] = both[k * BLK : (k + 1) * BLK]
            send_all(
                lambda to: back_buf.at[h, pl.ds(to * PER, PER)],
                adj_buf.at[it, h, pl.ds(me * PER, PER)],
                back_ss.at[h],
                back_rs.at[it, h],
            )

        def deposit():
            for b in range(BLOCKS):
                rows = slice(b * NVOX, (b + 1) * NVOX)
                field_out[pl.ds(b, NVOX, stride=BLOCKS), :] = jnp.where(
                    left(NVOX), dose[0, rows, :], dose[1, rows, :]
                )
            send_all(
                lambda to: field_out.at[pl.ds(vox_of(to) * BLOCKS, BLOCKS)],
                field_in.at[pl.ds(me * BLOCKS, BLOCKS)],
                field_ss,
                field_rs,
            )

        @pl.loop(0, PARTS)
        def _(h):
            wait(adj_buf.at[it, h], back_rs.at[it, h])
            for b in range(PER):
                high, low = halves(adj_buf[it, h, pl.ds(b, NDEV, stride=PER), :])
                value = jnp.concatenate([high, high, low], axis=0)
                near = left(BLK)
                for block, here in ((b, near), (PER + b, ~near)):
                    high, low = halves(jnp.where(here, dot(warp_t[block], value), 0.0))
                    rows = slice(place(block) * BLK, (place(block) + 1) * BLK)
                    la_cat[rows, :PLANS] = high
                    la_cat[rows, PLANS:] = low
            own = grad_in.at[it, h, pl.ds(chip * PACKED, PACKED)]
            order = (2, 1, 3, 0)

            def deliver(n):
                first = index(order[n] * 32) // 32
                layer = pl.multiple_of(first * (LAYER // 2), LAYER // 2)
                rows = pl.ds(layer, LAYER // 2)
                wait(pair_in.at[it, h, pl.ds(0, LAYER // 4)], pair_rs.at[it, h, n])
                grad_sum[h, rows, :] = grad[h, rows, :] + pair_in[it, h, rows, :]
                for o in CHIPS:
                    if o // 32 == order[n]:
                        to = index(o)
                        source = grad_sum.at[h, pl.ds(to * PACKED, PACKED)]
                        send(source, own, grad_ss.at[h], grad_rs.at[it, h], to)

            for n, dz in enumerate(order):
                first = index(dz * 32) // 32
                rows = pl.ds(pl.multiple_of(first * LAYER, LAYER), LAYER)
                part = joined(dot(tra_hi[rows, :], la_cat[...]))
                part = part + dot(tra_lo[rows, :], la_cat[:, :PLANS])
                flat[...] = part + swapped(part)
                even = flat[pl.ds(0, LAYER // 2, stride=2), :]
                odd = flat[pl.ds(1, LAYER // 2, stride=2), :]
                rows = pl.ds(pl.multiple_of(first * (LAYER // 2), LAYER // 2), LAYER // 2)
                grad[h, rows, :] = jnp.where(left(LAYER // 2), even, odd)
                for k in range(NVOX // 2):
                    device = first * NVOX + 2 * k + partner % 2
                    rows = pl.ds(device * PACKED, PACKED)
                    send(
                        grad.at[h, rows],
                        pair_in.at[it, h, rows],
                        pair_ss.at[h],
                        pair_rs.at[it, h, n],
                        partner,
                    )
                if n > 0:
                    deliver(n - 1)
                if n == DEPOSIT:
                    pl.when((it == ITERS - 1) & (h == 0))(deposit)
            deliver(len(order) - 1)
            source = grad_sum.at[h, pl.ds(me * PACKED, PACKED)]
            pltpu.make_async_copy(source, own, grad_rs.at[it, h]).start()

        @pl.when(it == ITERS - 1)
        def _():
            wait(field_in, field_rs)
            for b in range(BLOCKS):
                field[b * BLK : (b + 1) * BLK, :] = field_in[pl.ds(b, NDEV, stride=BLOCKS), :]
            stored.start()

        @pl.loop(0, PARTS)
        def _(h):
            wait(grad_in.at[it, h], grad_rs.at[it, h])
            for r in range(PACKED):
                total = jnp.sum(
                    grad_in[it, h, pl.ds(r, NCHIP, stride=PACKED), :], axis=0, keepdims=True
                )
                w_own[it + 1, h, r : r + 1, :] = jnp.maximum(
                    w_own[it, h, r : r + 1, :] - step_buf[pl.ds(h, 1), :] * total, 0.0
                )

            @pl.when(it < ITERS - 1)
            def _():
                share(it + 1, h)

        @pl.loop(0, PARTS)
        def _(h):
            wait(out_buf.at[h, pl.ds(0, (NDEV - 1) * PER)], out_ss.at[h])
            wait(back_buf.at[h, pl.ds(0, (NDEV - 1) * PER)], back_ss.at[h])
            wait(grad.at[h, pl.ds(0, (NCHIP - 1) * PACKED)], grad_ss.at[h])
            wait(grad.at[h, pl.ds(0, NCHIP * PACKED)], pair_ss.at[h])
            wait(w_buf.at[0, h, pl.ds(0, (NCHIP - 1) * PACKED)], w_ss.at[it, h])
            wait(w_buf.at[0, h, pl.ds(0, NCHIP * PACKED)], pass_ss.at[it, h])

    first, second = w_own[ITERS, 0, 0:PACKED, :], w_own[ITERS, 1, 0:PACKED, :]
    even = jnp.where(left(PACKED), first, swapped(second))
    odd = jnp.where(left(PACKED), swapped(first), second)
    for r in range(PACKED):
        new_weights[2 * r : 2 * r + 1, :] = even[r : r + 1, :]
        new_weights[2 * r + 1 : 2 * r + 2, :] = odd[r : r + 1, :]
    wait(info_in.at[pl.ds(0, NDEV - 1)], info_ss)
    wait(field_in.at[pl.ds(0, (NDEV - 1) * BLOCKS)], field_ss)
    stored.wait()


def finish(weights, field, new_weights, dose_field, small, large, in_sem, out_sem):
    pairs = [(weights, small, new_weights)]
    for n in range(4):
        rows = pl.ds(n * (ROWS // 4), ROWS // 4)
        pairs.append((field.at[rows], large.at[rows], dose_field.at[rows]))
    reads = [pltpu.make_async_copy(a, b, in_sem.at[n]) for n, (a, b, _) in enumerate(pairs)]
    writes = [pltpu.make_async_copy(b, c, out_sem.at[n]) for n, (_, b, c) in enumerate(pairs)]
    for read in reads:
        read.start()
    for read, write in zip(reads, writes):
        read.wait()
        write.start()
    for write in writes:
        write.wait()


def per_device(
    influence,
    weights,
    warp_tiles,
    owners,
    owner_slot,
    tile_index,
    structure,
    prescribed,
    importance,
    step_size,
):
    vmem = pl.BlockSpec(memory_space=pltpu.VMEM)
    smem = pl.BlockSpec(memory_space=pltpu.SMEM)
    hbm = pl.BlockSpec(memory_space=pl.ANY)
    dma = pltpu.SemaphoreType.DMA
    scratch = [
        pltpu.VMEM((4, LOAD, SPOTS), F32),
        pltpu.VMEM((ROWS, SPOTS), BF16),
        pltpu.VMEM((ROWS, SPOTS), BF16),
        pltpu.VMEM((SPOTS, ROWS), BF16),
        pltpu.VMEM((SPOTS, ROWS), BF16),
        pltpu.VMEM((NTILE, BLK, BLK), F32),
        pltpu.VMEM((BLOCKS, BLK, 3 * BLK), BF16),
        pltpu.VMEM((BLOCKS, BLK, 3 * BLK), BF16),
        pltpu.VMEM((BLK, BLK), F32),
        pltpu.VMEM((BLK, BLK), F32),
        pltpu.VMEM((TARGETS, SOURCES), BF16),
        pltpu.VMEM((SOURCES, TARGETS), BF16),
        pltpu.VMEM((ITERS, PARTS, SPOTS // 2, PLANS), F32),
        pltpu.VMEM((SPOTS, PLANS), F32),
        pltpu.VMEM((SPOTS, 2 * PLANS), BF16),
        pltpu.VMEM((ITERS + 1, PARTS, 8, PLANS), F32),
        pltpu.VMEM((8, PLANS), F32),
        pltpu.VMEM((PARTS, NDEV * PER, PLANS), F32),
        pltpu.VMEM((ITERS, PARTS, NDEV * PER, PLANS), F32),
        pltpu.VMEM((NDEV * PER, 2 * PLANS), BF16),
        pltpu.VMEM((PARTS, TARGETS, PLANS), F32),
        pltpu.VMEM((PARTS, TARGETS, PLANS), F32),
        pltpu.VMEM((TARGETS, PLANS), F32),
        pltpu.VMEM((TARGETS, 2 * PLANS), BF16),
        pltpu.VMEM((PARTS, NDEV * PER, PLANS), F32),
        pltpu.VMEM((ITERS, PARTS, NDEV * PER, PLANS), F32),
        pltpu.VMEM((ROWS, 2 * PLANS), BF16),
        pltpu.VMEM((LAYER, PLANS), F32),
        pltpu.VMEM((PARTS, SPOTS // 2, PLANS), F32),
        pltpu.VMEM((ITERS, PARTS, SPOTS // 2, PLANS), F32),
        pltpu.VMEM((PARTS, SPOTS // 2, PLANS), F32),
        pltpu.VMEM((ITERS, PARTS, NCHIP * PACKED, PLANS), F32),
        pltpu.VMEM((NVOX * BLOCKS, PLANS), F32),
        pltpu.VMEM((NDEV * BLOCKS, PLANS), F32),
        pltpu.VMEM((ROWS, PLANS), F32),
        dma((4,)),
        dma,
        dma,
        dma,
        dma((ITERS, PARTS)),
        dma((ITERS, PARTS)),
        dma((ITERS, PARTS)),
        dma((ITERS, PARTS)),
        dma((PARTS,)),
        dma((ITERS, PARTS)),
        dma((PARTS,)),
        dma((ITERS, PARTS)),
        dma((PARTS,)),
        dma((ITERS, PARTS, 4)),
        dma((PARTS,)),
        dma((ITERS, PARTS)),
        dma,
        dma,
    ]
    outs = (
        jax.ShapeDtypeStruct((OWN, PLANS), F32),
        jax.ShapeDtypeStruct((ROWS, PLANS), F32),
    )
    final_weights, field = pl.pallas_call(
        kernel,
        out_shape=outs,
        in_specs=[smem, smem, hbm, vmem, hbm, vmem, vmem, vmem, vmem, vmem],
        out_specs=(vmem, hbm),
        scratch_shapes=scratch,
        compiler_params=pltpu.CompilerParams(
            collective_id=0, has_side_effects=True, vmem_limit_bytes=67043328
        ),
    )(
        tile_index,
        importance.reshape(1, NSTRUCT),
        influence,
        weights,
        warp_tiles,
        owners.reshape(1, BLOCKS),
        owner_slot,
        structure.reshape(BLOCKS, BLK),
        prescribed,
        step_size.reshape(1, PLANS),
    )
    return pl.pallas_call(
        finish,
        out_shape=outs,
        in_specs=[hbm, hbm],
        out_specs=(hbm, hbm),
        scratch_shapes=[
            pltpu.VMEM((OWN, PLANS), F32),
            pltpu.VMEM((ROWS, PLANS), F32),
            dma((5,)),
            dma((5,)),
        ],
    )(final_weights, field)


def solution(mesh):
    split = Mesh(mesh.devices.reshape(SIZES), AXES)
    both = P("z", VOX)
    placed = (
        P("z", VOX, None),
        P(AXES, None),
        P(),
        P("z", VOX, None),
        both,
        both,
        P(VOX),
        P(),
        P(),
        P(),
    )
    return jax.shard_map(
        per_device,
        mesh=split,
        in_specs=placed,
        out_specs=(P(AXES, None), P(VOX, None)),
        check_vma=False,
    )
```

```python
import jax
import jax.numpy as jnp
from jax import lax
from jax.experimental import pallas as pl
from jax.experimental.pallas import tpu as pltpu
from jax.sharding import Mesh
from jax.sharding import PartitionSpec as P

AXES = ("z", "x", "y", "c")
VOX = ("x", "y", "c")
SIZES = (4, 4, 4, 2)
NDEV = 128
NVOX = 32
NSTRUCT = 8
ITERS = 2
PLANS = 128
BLK = 128
BLOCKS = 16
PARTS = 2
PER = BLOCKS // PARTS
SPOTS = 1536
OWN = SPOTS // NDEV
PACKED = OWN // PARTS
ROWS = BLOCKS * BLK
TARGETS = NVOX * BLOCKS
SOURCES = NDEV * BLOCKS
NTILE = 64
LOAD = 256
LOADS = ROWS // LOAD
GROUP = 512
DEPOSIT = 0
LATE = 2
PLANE = NVOX * BLOCKS
EARLY = 3
PAIR = GROUP // 2
LAYER = SPOTS // 4
LOGICAL = pl.DeviceIdType.LOGICAL
F32 = jnp.float32
BF16 = jnp.bfloat16


def offset_parts(offset):
    return offset // 32, (offset // 8) % 4, (offset // 2) % 4, offset % 2


def hops(offset):
    z, x, y, c = offset_parts(offset)
    return 2 * (min(z, 4 - z) + min(x, 4 - x) + min(y, 4 - y)) + c


OFFSETS = sorted(range(1, NDEV), key=lambda o: -hops(o))
CHIPS = [o for o in OFFSETS if o % 2 == 0]
NCHIP = NDEV // 2


def peers():
    z, x, y, c = [lax.axis_index(a) for a in AXES]
    pz = [lax.rem(z + d, 4) * 32 for d in range(4)]
    px = [lax.rem(x + d, 4) * 8 for d in range(4)]
    py = [lax.rem(y + d, 4) * 2 for d in range(4)]
    pc = [lax.rem(c + d, 2) for d in range(2)]
    zx = [[pz[a] + px[b] for b in range(4)] for a in range(4)]
    yc = [[py[a] + pc[b] for b in range(2)] for a in range(4)]

    def index(offset):
        dz, dx, dy, dc = offset_parts(offset)
        return zx[dz][dx] + yc[dy][dc]

    return index


def halves(value):
    high = value.astype(BF16)
    low = (value - high.astype(F32)).astype(BF16)
    return high, low


def dot(a, b):
    return jnp.dot(a, b, preferred_element_type=F32)


def left(rows):
    return lax.broadcasted_iota(jnp.int32, (rows, PLANS), 1) < PLANS // 2


def swapped(value):
    return pltpu.roll(value, PLANS // 2, 1)


def joined(pair):
    return pair[:, :PLANS] + pair[:, PLANS:]


def kernel(
    tile_ids,
    importance,
    influence,
    weights,
    tiles,
    owners,
    slots,
    structure,
    prescribed,
    step,
    new_weights,
    dose_out,
    staged,
    mat_hi,
    mat_lo,
    tra_hi,
    tra_lo,
    tile_buf,
    warp,
    warp_t,
    info_out,
    info_in,
    gather_in,
    gather_t,
    w_buf,
    w_flat,
    w_cat,
    w_own,
    step_buf,
    out_buf,
    in_buf,
    in_cat,
    dose,
    target_dose,
    voxel_weight,
    adj_cat,
    back_buf,
    adj_buf,
    la_cat,
    flat,
    grad,
    pair_in,
    grad_sum,
    grad_in,
    field_out,
    field_in,
    field,
    load_sem,
    tile_sem,
    info_ss,
    info_rs,
    w_ss,
    w_rs,
    pass_ss,
    pass_rs,
    out_ss,
    out_rs,
    back_ss,
    back_rs,
    pair_ss,
    pair_rs,
    grad_ss,
    grad_rs,
    field_ss,
    field_rs,
    relay_ss,
    relay_rs,
):
    index = peers()
    me = index(0)
    partner = index(1)
    chip = me // 2
    vox_of = lambda device: lax.rem(device, NVOX)

    def send(src, dst, send_sem, recv_sem, to):
        pltpu.make_async_remote_copy(
            src_ref=src,
            dst_ref=dst,
            send_sem=send_sem,
            recv_sem=recv_sem,
            device_id=to,
            device_id_type=LOGICAL,
        ).start()

    def send_all(src, dst, send_sem, recv_sem):
        for o in OFFSETS:
            send(src(index(o)), dst, send_sem, recv_sem, index(o))
        pltpu.make_async_copy(src(me), dst, recv_sem).start()

    def wait(ref, sem):
        pltpu.make_async_copy(ref, ref, sem).wait()

    stored = pltpu.make_async_copy(field, dose_out, tile_sem)
    loads = []
    for n in range(LOADS):
        loads.append(
            pltpu.make_async_copy(
                influence.at[0, pl.ds(n * LOAD, LOAD)], staged.at[n % 4], load_sem.at[n % 4]
            )
        )
    for n in range(4):
        loads[n].start()
    tile_load = pltpu.make_async_copy(tiles, tile_buf, tile_sem)
    tile_load.start()

    barrier = pltpu.get_barrier_semaphore()
    for o in OFFSETS:
        pl.semaphore_signal(barrier, inc=1, device_id=index(o), device_id_type=LOGICAL)

    info_out[...] = jnp.zeros((BLK, BLK), F32)
    info_out[BLOCKS : 2 * BLOCKS, :] = structure[...].astype(F32)
    turned = info_out[...].T
    flat[0:1, 0:BLOCKS] = (slots[...] * NVOX + owners[...]).astype(F32)
    lane = lax.broadcasted_iota(jnp.int32, (BLK, BLK), 1)
    info_out[...] = jnp.where(lane < BLOCKS, flat[0:1, :], turned)

    def place(b):
        return 2 * (b % PER) + b // PER

    def convert(n):
        loads[n].wait()

        @pl.loop(0, SPOTS // BLK)
        def _(k):
            cols = pl.ds(pl.multiple_of(k * BLK, BLK), BLK)
            for h in range(LOAD // BLK):
                high, low = halves(staged[n % 4, h * BLK : (h + 1) * BLK, cols])
                rows = pl.ds(place(n * (LOAD // BLK) + h) * BLK, BLK)
                mat_hi[rows, cols] = high
                mat_lo[rows, cols] = low

        if n + 4 < LOADS:
            loads[n + 4].start()

    for n in range(EARLY):
        convert(n)

    even = weights[pl.ds(0, PACKED, stride=2), :]
    odd = weights[pl.ds(1, PACKED, stride=2), :]
    w_own[0, 0, 0:PACKED, :] = jnp.where(left(PACKED), even, swapped(odd))
    w_own[0, 1, 0:PACKED, :] = jnp.where(left(PACKED), swapped(even), odd)
    step_buf[0:1, :] = jnp.where(left(1), step[...], swapped(step[...]))
    step_buf[1:2, :] = jnp.where(left(1), swapped(step[...]), step[...])
    pl.semaphore_wait(barrier, NDEV - 1)

    def share(it, h):
        source = w_own.at[it, h, pl.ds(0, PACKED)]
        own = w_buf.at[it, h, pl.ds(me * PACKED, PACKED)]
        for o in CHIPS:
            send(source, own, w_ss.at[it, h], w_rs.at[it, h], index(o))
        pltpu.make_async_copy(source, own, w_rs.at[it, h]).start()

    def forward(it, h):
        wait(w_buf.at[it, h, pl.ds(0, NCHIP * PACKED)], w_rs.at[it, h])
        for k in range(NCHIP):
            rows = w_buf.at[it, h, pl.ds((2 * k + me % 2) * PACKED, PACKED)]
            send(rows, rows, pass_ss.at[it, h], pass_rs.at[it, h], partner)

    send_all(
        lambda to: info_out.at[pl.ds(to, 1)], info_in.at[pl.ds(me, 1)], info_ss, info_rs
    )
    share(0, 0)
    share(0, 1)
    for n in range(EARLY, LOADS):
        convert(n)
    tile_load.wait()

    @pl.loop(0, BLOCKS)
    def _(b):
        tile = tile_buf[tile_ids[0, b]]
        high, low = halves(tile)
        warp[b, :, 0:BLK] = high
        warp[b, :, BLK : 2 * BLK] = low
        warp[b, :, 2 * BLK :] = high
        high, low = halves(tile.T)
        warp_t[b, :, 0:BLK] = high
        warp_t[b, :, BLK : 2 * BLK] = low
        warp_t[b, :, 2 * BLK :] = high

    def turn(h):
        @pl.loop(0, SPOTS // BLK // PARTS)
        def _(k):
            cols = pl.ds(pl.multiple_of(h * (SPOTS // PARTS) + k * BLK, BLK), BLK)
            for n in range(ROWS // GROUP):
                rows = slice(n * GROUP, (n + 1) * GROUP)
                tra_hi[cols, rows] = mat_hi[rows, cols].T
                tra_lo[cols, rows] = mat_lo[rows, cols].T

    def warped(matrix, value):
        high, low = halves(value)
        return dot(matrix, jnp.concatenate([high, high, low], axis=0))

    def tables():
        wait(info_in, info_rs)
        info = info_in[...]
        turned = info.T
        down = lax.broadcasted_iota(jnp.int32, (BLK, BLK), 0).astype(F32)
        across = lax.broadcasted_iota(jnp.int32, (1, BLK), 1).astype(F32)
        for b in range(BLOCKS):
            at = slice(b * BLK, (b + 1) * BLK)
            row, column = turned[b : b + 1, :], info[:, b : b + 1]
            for n in range(TARGETS // BLK):
                to = slice(n * BLK, (n + 1) * BLK)
                hit = down == row - float(n * BLK)
                gather_in[to, at] = jnp.where(hit, 1.0, 0.0).astype(BF16)
                hit = column == across + float(n * BLK)
                gather_t[at, to] = jnp.where(hit, 1.0, 0.0).astype(BF16)
            kind = info[0:NVOX, BLOCKS + b : BLOCKS + b + 1]
            goal = jnp.zeros((NVOX, PLANS), F32)
            scale = jnp.zeros((NVOX, PLANS), F32)
            for s in range(NSTRUCT):
                goal = jnp.where(kind == float(s), prescribed[s : s + 1, :], goal)
                scale = jnp.where(kind == float(s), importance[0, s], scale)
            at = slice(b * NVOX, (b + 1) * NVOX)
            target_dose[0, at, :] = jnp.where(left(NVOX), goal, swapped(goal))
            target_dose[1, at, :] = jnp.where(left(NVOX), swapped(goal), goal)
            voxel_weight[at, :] = scale

    forward(0, 0)
    tables()

    @pl.loop(0, ITERS)
    def _(it):
        @pl.loop(0, PARTS)
        def _(h):
            pl.when((it > 0) & (h == 0))(lambda: forward(it, h))
            wait(w_buf.at[it, h, pl.ds(0, NCHIP * PACKED)], pass_rs.at[it, h])
            pair = w_buf[it, h]
            turned = swapped(pair)
            near = left(SPOTS // 2)
            w_flat[pl.ds(0, SPOTS // 2, stride=2), :] = jnp.where(near, pair, turned)
            w_flat[pl.ds(1, SPOTS // 2, stride=2), :] = jnp.where(near, turned, pair)
            high, low = halves(w_flat[...])
            w_cat[:, :PLANS] = high
            w_cat[:, PLANS:] = low

            @pl.loop(0, ROWS // GROUP)
            def _(g):
                pl.when((g == LATE) & (h == 0))(lambda: forward(it, 1))
                rows = pl.ds(pl.multiple_of(g * GROUP, GROUP), GROUP)
                part = joined(dot(mat_hi[rows, :], w_cat[...]))
                part = part + dot(mat_lo[rows, :], w_cat[:, :PLANS])
                for k in range(PAIR // BLK):
                    b = g * (PAIR // BLK) + k
                    at = 2 * k * BLK
                    first = warped(warp[b], part[at : at + BLK])
                    second = warped(warp[PER + b], part[at + BLK : at + 2 * BLK])
                    out_buf[h, pl.ds(b, NDEV, stride=PER), :] = jnp.where(left(BLK), first, second)

            send_all(
                lambda to: out_buf.at[h, pl.ds(to * PER, PER)],
                in_buf.at[it, h, pl.ds(me * PER, PER)],
                out_ss.at[h],
                out_rs.at[it, h],
            )

        @pl.loop(0, PARTS)
        def _(h):
            pl.when(it == 0)(lambda: turn(h))
            wait(in_buf.at[it, h], out_rs.at[it, h])
            for b in range(PER):
                high, low = halves(in_buf[it, h, pl.ds(b, NDEV, stride=PER), :])
                in_cat[b * NDEV : (b + 1) * NDEV, :PLANS] = high
                in_cat[b * NDEV : (b + 1) * NDEV, PLANS:] = low
            near = left(TARGETS)
            total = jnp.where(
                near,
                joined(dot(gather_in[:, : PER * NDEV], in_cat[...])),
                joined(dot(gather_in[:, PER * NDEV :], in_cat[...])),
            )
            total = total + swapped(total)
            dose[h] = total
            high, low = halves(voxel_weight[...] * (total - target_dose[h]))
            adj_cat[:, :PLANS] = high
            adj_cat[:, PLANS:] = low
            for b in range(0, PER, PAIR // BLK):
                first = joined(dot(gather_t[b * NDEV : b * NDEV + PAIR, :], adj_cat[...]))
                second = (PER + b) * NDEV
                second = joined(dot(gather_t[second : second + PAIR, :], adj_cat[...]))
                both = jnp.where(left(PAIR), first, second)
                for k in range(PAIR // BLK):
                    back_buf[h, pl.ds(b + k, NDEV, stride=PER), :] = both[k * BLK : (k + 1) * BLK]
            send_all(
                lambda to: back_buf.at[h, pl.ds(to * PER, PER)],
                adj_buf.at[it, h, pl.ds(me * PER, PER)],
                back_ss.at[h],
                back_rs.at[it, h],
            )

        def deposit():
            for b in range(BLOCKS):
                rows = slice(b * NVOX, (b + 1) * NVOX)
                field_out[pl.ds(b, NVOX, stride=BLOCKS), :] = jnp.where(
                    left(NVOX), dose[0, rows, :], dose[1, rows, :]
                )
            own = field_in.at[pl.ds(me * BLOCKS, BLOCKS)]
            for o in OFFSETS:
                if o // 32 != 2:
                    source = field_out.at[pl.ds(vox_of(index(o)) * BLOCKS, BLOCKS)]
                    send(source, own, field_ss, field_rs.at[o // 32], index(o))
            source = field_out.at[pl.ds(vox_of(me) * BLOCKS, BLOCKS)]
            pltpu.make_async_copy(source, own, field_rs.at[0]).start()

        def plane(dz):
            return pl.multiple_of(index(dz * 32) // 32 * PLANE, PLANE)

        def relay():
            wait(field_in.at[pl.ds(plane(3), PLANE)], field_rs.at[1])
            rows = field_in.at[pl.ds(plane(3), PLANE // 2)]
            send(rows, rows, relay_ss.at[0], relay_rs.at[0], index(32))
            wait(field_in.at[pl.ds(plane(1), PLANE)], field_rs.at[3])
            rows = field_in.at[pl.ds(plane(1) + PLANE // 2, PLANE // 2)]
            send(rows, rows, relay_ss.at[1], relay_rs.at[1], index(96))

        @pl.loop(0, PARTS)
        def _(h):
            wait(adj_buf.at[it, h], back_rs.at[it, h])
            for b in range(PER):
                high, low = halves(adj_buf[it, h, pl.ds(b, NDEV, stride=PER), :])
                value = jnp.concatenate([high, high, low], axis=0)
                near = left(BLK)
                for block, here in ((b, near), (PER + b, ~near)):
                    high, low = halves(jnp.where(here, dot(warp_t[block], value), 0.0))
                    rows = slice(place(block) * BLK, (place(block) + 1) * BLK)
                    la_cat[rows, :PLANS] = high
                    la_cat[rows, PLANS:] = low
            own = grad_in.at[it, h, pl.ds(chip * PACKED, PACKED)]
            order = (2, 1, 3, 0)

            def deliver(n):
                first = index(order[n] * 32) // 32
                layer = pl.multiple_of(first * (LAYER // 2), LAYER // 2)
                rows = pl.ds(layer, LAYER // 2)
                wait(pair_in.at[it, h, pl.ds(0, LAYER // 4)], pair_rs.at[it, h, n])
                grad_sum[h, rows, :] = grad[h, rows, :] + pair_in[it, h, rows, :]
                for o in CHIPS:
                    if o // 32 == order[n]:
                        to = index(o)
                        source = grad_sum.at[h, pl.ds(to * PACKED, PACKED)]
                        send(source, own, grad_ss.at[h], grad_rs.at[it, h], to)

            for n, dz in enumerate(order):
                first = index(dz * 32) // 32
                rows = pl.ds(pl.multiple_of(first * LAYER, LAYER), LAYER)
                part = joined(dot(tra_hi[rows, :], la_cat[...]))
                part = part + dot(tra_lo[rows, :], la_cat[:, :PLANS])
                flat[...] = part + swapped(part)
                even = flat[pl.ds(0, LAYER // 2, stride=2), :]
                odd = flat[pl.ds(1, LAYER // 2, stride=2), :]
                rows = pl.ds(pl.multiple_of(first * (LAYER // 2), LAYER // 2), LAYER // 2)
                grad[h, rows, :] = jnp.where(left(LAYER // 2), even, odd)
                for k in range(NVOX // 2):
                    device = first * NVOX + 2 * k + partner % 2
                    rows = pl.ds(device * PACKED, PACKED)
                    send(
                        grad.at[h, rows],
                        pair_in.at[it, h, rows],
                        pair_ss.at[h],
                        pair_rs.at[it, h, n],
                        partner,
                    )
                if n > 0:
                    deliver(n - 1)
                if n == DEPOSIT:
                    pl.when((it == ITERS - 1) & (h == 0))(deposit)
            deliver(len(order) - 1)
            source = grad_sum.at[h, pl.ds(me * PACKED, PACKED)]
            pltpu.make_async_copy(source, own, grad_rs.at[it, h]).start()

        @pl.when(it == ITERS - 1)
        def _():
            relay()
            wait(field_in.at[pl.ds(plane(0), PLANE)], field_rs.at[0])
            for k in range(2):
                half = field_in.at[pl.ds(plane(2) + k * (PLANE // 2), PLANE // 2)]
                wait(half, relay_rs.at[k])
            for b in range(BLOCKS):
                field[b * BLK : (b + 1) * BLK, :] = field_in[pl.ds(b, NDEV, stride=BLOCKS), :]
            stored.start()

        @pl.loop(0, PARTS)
        def _(h):
            wait(grad_in.at[it, h], grad_rs.at[it, h])
            for r in range(PACKED):
                total = jnp.sum(
                    grad_in[it, h, pl.ds(r, NCHIP, stride=PACKED), :], axis=0, keepdims=True
                )
                w_own[it + 1, h, r : r + 1, :] = jnp.maximum(
                    w_own[it, h, r : r + 1, :] - step_buf[pl.ds(h, 1), :] * total, 0.0
                )

            @pl.when(it < ITERS - 1)
            def _():
                share(it + 1, h)

        @pl.loop(0, PARTS)
        def _(h):
            wait(out_buf.at[h, pl.ds(0, (NDEV - 1) * PER)], out_ss.at[h])
            wait(back_buf.at[h, pl.ds(0, (NDEV - 1) * PER)], back_ss.at[h])
            wait(grad.at[h, pl.ds(0, (NCHIP - 1) * PACKED)], grad_ss.at[h])
            wait(grad.at[h, pl.ds(0, NCHIP * PACKED)], pair_ss.at[h])
            wait(w_buf.at[0, h, pl.ds(0, (NCHIP - 1) * PACKED)], w_ss.at[it, h])
            wait(w_buf.at[0, h, pl.ds(0, NCHIP * PACKED)], pass_ss.at[it, h])

    first, second = w_own[ITERS, 0, 0:PACKED, :], w_own[ITERS, 1, 0:PACKED, :]
    even = jnp.where(left(PACKED), first, swapped(second))
    odd = jnp.where(left(PACKED), swapped(first), second)
    for r in range(PACKED):
        new_weights[2 * r : 2 * r + 1, :] = even[r : r + 1, :]
        new_weights[2 * r + 1 : 2 * r + 2, :] = odd[r : r + 1, :]
    wait(info_in.at[pl.ds(0, NDEV - 1)], info_ss)
    wait(field_in.at[pl.ds(0, 3 * PLANE - BLOCKS)], field_ss)
    for k in range(2):
        wait(field_in.at[pl.ds(0, PLANE // 2)], relay_ss.at[k])
    stored.wait()


def finish(weights, field, new_weights, dose_field, small, large, in_sem, out_sem):
    pairs = [(weights, small, new_weights)]
    for n in range(4):
        rows = pl.ds(n * (ROWS // 4), ROWS // 4)
        pairs.append((field.at[rows], large.at[rows], dose_field.at[rows]))
    reads = [pltpu.make_async_copy(a, b, in_sem.at[n]) for n, (a, b, _) in enumerate(pairs)]
    writes = [pltpu.make_async_copy(b, c, out_sem.at[n]) for n, (_, b, c) in enumerate(pairs)]
    for read in reads:
        read.start()
    for read, write in zip(reads, writes):
        read.wait()
        write.start()
    for write in writes:
        write.wait()


def per_device(
    influence,
    weights,
    warp_tiles,
    owners,
    owner_slot,
    tile_index,
    structure,
    prescribed,
    importance,
    step_size,
):
    vmem = pl.BlockSpec(memory_space=pltpu.VMEM)
    smem = pl.BlockSpec(memory_space=pltpu.SMEM)
    hbm = pl.BlockSpec(memory_space=pl.ANY)
    dma = pltpu.SemaphoreType.DMA
    scratch = [
        pltpu.VMEM((4, LOAD, SPOTS), F32),
        pltpu.VMEM((ROWS, SPOTS), BF16),
        pltpu.VMEM((ROWS, SPOTS), BF16),
        pltpu.VMEM((SPOTS, ROWS), BF16),
        pltpu.VMEM((SPOTS, ROWS), BF16),
        pltpu.VMEM((NTILE, BLK, BLK), F32),
        pltpu.VMEM((BLOCKS, BLK, 3 * BLK), BF16),
        pltpu.VMEM((BLOCKS, BLK, 3 * BLK), BF16),
        pltpu.VMEM((BLK, BLK), F32),
        pltpu.VMEM((BLK, BLK), F32),
        pltpu.VMEM((TARGETS, SOURCES), BF16),
        pltpu.VMEM((SOURCES, TARGETS), BF16),
        pltpu.VMEM((ITERS, PARTS, SPOTS // 2, PLANS), F32),
        pltpu.VMEM((SPOTS, PLANS), F32),
        pltpu.VMEM((SPOTS, 2 * PLANS), BF16),
        pltpu.VMEM((ITERS + 1, PARTS, 8, PLANS), F32),
        pltpu.VMEM((8, PLANS), F32),
        pltpu.VMEM((PARTS, NDEV * PER, PLANS), F32),
        pltpu.VMEM((ITERS, PARTS, NDEV * PER, PLANS), F32),
        pltpu.VMEM((NDEV * PER, 2 * PLANS), BF16),
        pltpu.VMEM((PARTS, TARGETS, PLANS), F32),
        pltpu.VMEM((PARTS, TARGETS, PLANS), F32),
        pltpu.VMEM((TARGETS, PLANS), F32),
        pltpu.VMEM((TARGETS, 2 * PLANS), BF16),
        pltpu.VMEM((PARTS, NDEV * PER, PLANS), F32),
        pltpu.VMEM((ITERS, PARTS, NDEV * PER, PLANS), F32),
        pltpu.VMEM((ROWS, 2 * PLANS), BF16),
        pltpu.VMEM((LAYER, PLANS), F32),
        pltpu.VMEM((PARTS, SPOTS // 2, PLANS), F32),
        pltpu.VMEM((ITERS, PARTS, SPOTS // 2, PLANS), F32),
        pltpu.VMEM((PARTS, SPOTS // 2, PLANS), F32),
        pltpu.VMEM((ITERS, PARTS, NCHIP * PACKED, PLANS), F32),
        pltpu.VMEM((NVOX * BLOCKS, PLANS), F32),
        pltpu.VMEM((NDEV * BLOCKS, PLANS), F32),
        pltpu.VMEM((ROWS, PLANS), F32),
        dma((4,)),
        dma,
        dma,
        dma,
        dma((ITERS, PARTS)),
        dma((ITERS, PARTS)),
        dma((ITERS, PARTS)),
        dma((ITERS, PARTS)),
        dma((PARTS,)),
        dma((ITERS, PARTS)),
        dma((PARTS,)),
        dma((ITERS, PARTS)),
        dma((PARTS,)),
        dma((ITERS, PARTS, 4)),
        dma((PARTS,)),
        dma((ITERS, PARTS)),
        dma,
        dma((4,)),
        dma((2,)),
        dma((2,)),
    ]
    outs = (
        jax.ShapeDtypeStruct((OWN, PLANS), F32),
        jax.ShapeDtypeStruct((ROWS, PLANS), F32),
    )
    final_weights, field = pl.pallas_call(
        kernel,
        out_shape=outs,
        in_specs=[smem, smem, hbm, vmem, hbm, vmem, vmem, vmem, vmem, vmem],
        out_specs=(vmem, hbm),
        scratch_shapes=scratch,
        compiler_params=pltpu.CompilerParams(
            collective_id=0, has_side_effects=True, vmem_limit_bytes=67043328
        ),
    )(
        tile_index,
        importance.reshape(1, NSTRUCT),
        influence,
        weights,
        warp_tiles,
        owners.reshape(1, BLOCKS),
        owner_slot,
        structure.reshape(BLOCKS, BLK),
        prescribed,
        step_size.reshape(1, PLANS),
    )
    return pl.pallas_call(
        finish,
        out_shape=outs,
        in_specs=[hbm, hbm],
        out_specs=(hbm, hbm),
        scratch_shapes=[
            pltpu.VMEM((OWN, PLANS), F32),
            pltpu.VMEM((ROWS, PLANS), F32),
            dma((5,)),
            dma((5,)),
        ],
    )(final_weights, field)


def solution(mesh):
    split = Mesh(mesh.devices.reshape(SIZES), AXES)
    both = P("z", VOX)
    placed = (
        P("z", VOX, None),
        P(AXES, None),
        P(),
        P("z", VOX, None),
        both,
        both,
        P(VOX),
        P(),
        P(),
        P(),
    )
    return jax.shard_map(
        per_device,
        mesh=split,
        in_specs=placed,
        out_specs=(P(AXES, None), P(VOX, None)),
        check_vma=False,
    )
```

```python
import jax
import jax.numpy as jnp
from jax import lax
from jax.experimental import pallas as pl
from jax.experimental.pallas import tpu as pltpu
from jax.sharding import Mesh
from jax.sharding import PartitionSpec as P

AXES = ("z", "x", "y", "c")
VOX = ("x", "y", "c")
SIZES = (4, 4, 4, 2)
NDEV = 128
NVOX = 32
NSTRUCT = 8
ITERS = 2
PLANS = 128
BLK = 128
BLOCKS = 16
PARTS = 2
PER = BLOCKS // PARTS
SPOTS = 1536
OWN = SPOTS // NDEV
PACKED = OWN // PARTS
ROWS = BLOCKS * BLK
TARGETS = NVOX * BLOCKS
SOURCES = NDEV * BLOCKS
NTILE = 64
LOAD = 256
LOADS = ROWS // LOAD
GROUP = 512
DEPOSIT = 0
LATE = 2
PLANE = NVOX * BLOCKS
EARLY = 3
PAIR = GROUP // 2
LAYER = SPOTS // 4
LOGICAL = pl.DeviceIdType.LOGICAL
F32 = jnp.float32
BF16 = jnp.bfloat16


def offset_parts(offset):
    return offset // 32, (offset // 8) % 4, (offset // 2) % 4, offset % 2


def hops(offset):
    z, x, y, c = offset_parts(offset)
    return 2 * (min(z, 4 - z) + min(x, 4 - x) + min(y, 4 - y)) + c


OFFSETS = sorted(range(1, NDEV), key=lambda o: -hops(o))
CHIPS = [o for o in OFFSETS if o % 2 == 0]
NCHIP = NDEV // 2


def peers():
    z, x, y, c = [lax.axis_index(a) for a in AXES]
    pz = [lax.rem(z + d, 4) * 32 for d in range(4)]
    px = [lax.rem(x + d, 4) * 8 for d in range(4)]
    py = [lax.rem(y + d, 4) * 2 for d in range(4)]
    pc = [lax.rem(c + d, 2) for d in range(2)]
    zx = [[pz[a] + px[b] for b in range(4)] for a in range(4)]
    yc = [[py[a] + pc[b] for b in range(2)] for a in range(4)]

    def index(offset):
        dz, dx, dy, dc = offset_parts(offset)
        return zx[dz][dx] + yc[dy][dc]

    return index


def halves(value):
    high = value.astype(BF16)
    low = (value - high.astype(F32)).astype(BF16)
    return high, low


def dot(a, b):
    return jnp.dot(a, b, preferred_element_type=F32)


def left(rows):
    return lax.broadcasted_iota(jnp.int32, (rows, PLANS), 1) < PLANS // 2


def swapped(value):
    return pltpu.roll(value, PLANS // 2, 1)


def joined(pair):
    return pair[:, :PLANS] + pair[:, PLANS:]


def kernel(
    tile_ids,
    importance,
    influence,
    weights,
    tiles,
    owners,
    slots,
    structure,
    prescribed,
    step,
    new_weights,
    dose_out,
    staged,
    mat_hi,
    mat_lo,
    tra_hi,
    tra_lo,
    tile_buf,
    warp,
    warp_t,
    info_out,
    info_in,
    gather_in,
    gather_t,
    w_buf,
    w_flat,
    w_cat,
    w_own,
    step_buf,
    out_buf,
    in_buf,
    in_cat,
    dose,
    target_dose,
    voxel_weight,
    adj_cat,
    back_buf,
    adj_buf,
    la_cat,
    flat,
    grad,
    pair_in,
    grad_sum,
    grad_in,
    field_out,
    field_in,
    field,
    load_sem,
    tile_sem,
    info_ss,
    info_rs,
    w_ss,
    w_rs,
    pass_ss,
    pass_rs,
    out_ss,
    out_rs,
    back_ss,
    back_rs,
    pair_ss,
    pair_rs,
    grad_ss,
    grad_rs,
    field_ss,
    field_rs,
    relay_ss,
    relay_rs,
):
    index = peers()
    me = index(0)
    partner = index(1)
    chip = me // 2
    vox_of = lambda device: lax.rem(device, NVOX)

    def send(src, dst, send_sem, recv_sem, to):
        pltpu.make_async_remote_copy(
            src_ref=src,
            dst_ref=dst,
            send_sem=send_sem,
            recv_sem=recv_sem,
            device_id=to,
            device_id_type=LOGICAL,
        ).start()

    def send_all(src, dst, send_sem, recv_sem):
        for o in OFFSETS:
            send(src(index(o)), dst, send_sem, recv_sem, index(o))
        pltpu.make_async_copy(src(me), dst, recv_sem).start()

    def wait(ref, sem):
        pltpu.make_async_copy(ref, ref, sem).wait()

    stored = pltpu.make_async_copy(field, dose_out, tile_sem)
    loads = []
    for n in range(LOADS):
        loads.append(
            pltpu.make_async_copy(
                influence.at[0, pl.ds(n * LOAD, LOAD)], staged.at[n % 4], load_sem.at[n % 4]
            )
        )
    for n in range(4):
        loads[n].start()
    tile_load = pltpu.make_async_copy(tiles, tile_buf, tile_sem)
    tile_load.start()

    barrier = pltpu.get_barrier_semaphore()
    for o in OFFSETS:
        pl.semaphore_signal(barrier, inc=1, device_id=index(o), device_id_type=LOGICAL)

    info_out[...] = jnp.zeros((BLK, BLK), F32)
    info_out[BLOCKS : 2 * BLOCKS, :] = structure[...].astype(F32)
    turned = info_out[...].T
    flat[0:1, 0:BLOCKS] = (slots[...] * NVOX + owners[...]).astype(F32)
    lane = lax.broadcasted_iota(jnp.int32, (BLK, BLK), 1)
    info_out[...] = jnp.where(lane < BLOCKS, flat[0:1, :], turned)

    def place(b):
        return 2 * (b % PER) + b // PER

    def convert(n):
        loads[n].wait()

        @pl.loop(0, SPOTS // BLK)
        def _(k):
            cols = pl.ds(pl.multiple_of(k * BLK, BLK), BLK)
            for h in range(LOAD // BLK):
                high, low = halves(staged[n % 4, h * BLK : (h + 1) * BLK, cols])
                rows = pl.ds(place(n * (LOAD // BLK) + h) * BLK, BLK)
                mat_hi[rows, cols] = high
                mat_lo[rows, cols] = low

        if n + 4 < LOADS:
            loads[n + 4].start()

    for n in range(EARLY):
        convert(n)

    even = weights[pl.ds(0, PACKED, stride=2), :]
    odd = weights[pl.ds(1, PACKED, stride=2), :]
    w_own[0, 0, 0:PACKED, :] = jnp.where(left(PACKED), even, swapped(odd))
    w_own[0, 1, 0:PACKED, :] = jnp.where(left(PACKED), swapped(even), odd)
    step_buf[0:1, :] = jnp.where(left(1), step[...], swapped(step[...]))
    step_buf[1:2, :] = jnp.where(left(1), swapped(step[...]), step[...])
    pl.semaphore_wait(barrier, NDEV - 1)

    def share(it, h):
        source = w_own.at[it, h, pl.ds(0, PACKED)]
        own = w_buf.at[it, h, pl.ds(me * PACKED, PACKED)]
        for o in CHIPS:
            send(source, own, w_ss.at[it, h], w_rs.at[it, h], index(o))
        pltpu.make_async_copy(source, own, w_rs.at[it, h]).start()

    def forward(it, h):
        wait(w_buf.at[it, h, pl.ds(0, NCHIP * PACKED)], w_rs.at[it, h])
        for k in range(NCHIP):
            rows = w_buf.at[it, h, pl.ds((2 * k + me % 2) * PACKED, PACKED)]
            send(rows, rows, pass_ss.at[it, h], pass_rs.at[it, h], partner)

    send_all(
        lambda to: info_out.at[pl.ds(to, 1)], info_in.at[pl.ds(me, 1)], info_ss, info_rs
    )
    share(0, 0)
    share(0, 1)
    for n in range(EARLY, LOADS):
        convert(n)
    tile_load.wait()

    @pl.loop(0, BLOCKS)
    def _(b):
        tile = tile_buf[tile_ids[0, b]]
        high, low = halves(tile)
        warp[b, :, 0:BLK] = high
        warp[b, :, BLK : 2 * BLK] = low
        warp[b, :, 2 * BLK :] = high
        high, low = halves(tile.T)
        warp_t[b, :, 0:BLK] = high
        warp_t[b, :, BLK : 2 * BLK] = low
        warp_t[b, :, 2 * BLK :] = high

    def turn(h):
        @pl.loop(0, SPOTS // BLK // PARTS)
        def _(k):
            cols = pl.ds(pl.multiple_of(h * (SPOTS // PARTS) + k * BLK, BLK), BLK)
            for n in range(ROWS // GROUP):
                rows = slice(n * GROUP, (n + 1) * GROUP)
                tra_hi[cols, rows] = mat_hi[rows, cols].T
                tra_lo[cols, rows] = mat_lo[rows, cols].T

    def warped(matrix, value):
        high, low = halves(value)
        return dot(matrix, jnp.concatenate([high, high, low], axis=0))

    def tables():
        wait(info_in, info_rs)
        info = info_in[...]
        turned = info.T
        down = lax.broadcasted_iota(jnp.int32, (BLK, BLK), 0).astype(F32)
        across = lax.broadcasted_iota(jnp.int32, (1, BLK), 1).astype(F32)
        for b in range(BLOCKS):
            at = slice(b * BLK, (b + 1) * BLK)
            row, column = turned[b : b + 1, :], info[:, b : b + 1]
            for n in range(TARGETS // BLK):
                to = slice(n * BLK, (n + 1) * BLK)
                hit = down == row - float(n * BLK)
                gather_in[to, at] = jnp.where(hit, 1.0, 0.0).astype(BF16)
                hit = column == across + float(n * BLK)
                gather_t[at, to] = jnp.where(hit, 1.0, 0.0).astype(BF16)
            kind = info[0:NVOX, BLOCKS + b : BLOCKS + b + 1]
            goal = jnp.zeros((NVOX, PLANS), F32)
            scale = jnp.zeros((NVOX, PLANS), F32)
            for s in range(NSTRUCT):
                goal = jnp.where(kind == float(s), prescribed[s : s + 1, :], goal)
                scale = jnp.where(kind == float(s), importance[0, s], scale)
            at = slice(b * NVOX, (b + 1) * NVOX)
            target_dose[0, at, :] = jnp.where(left(NVOX), goal, swapped(goal))
            target_dose[1, at, :] = jnp.where(left(NVOX), swapped(goal), goal)
            voxel_weight[at, :] = scale

    forward(0, 0)
    tables()

    @pl.loop(0, ITERS)
    def _(it):
        @pl.loop(0, PARTS)
        def _(h):
            pl.when((it > 0) & (h == 0))(lambda: forward(it, h))
            wait(w_buf.at[it, h, pl.ds(0, NCHIP * PACKED)], pass_rs.at[it, h])
            pair = w_buf[it, h]
            turned = swapped(pair)
            near = left(SPOTS // 2)
            w_flat[pl.ds(0, SPOTS // 2, stride=2), :] = jnp.where(near, pair, turned)
            w_flat[pl.ds(1, SPOTS // 2, stride=2), :] = jnp.where(near, turned, pair)
            high, low = halves(w_flat[...])
            w_cat[:, :PLANS] = high
            w_cat[:, PLANS:] = low

            @pl.loop(0, ROWS // GROUP)
            def _(g):
                pl.when((g == LATE) & (h == 0))(lambda: forward(it, 1))
                rows = pl.ds(pl.multiple_of(g * GROUP, GROUP), GROUP)
                part = joined(dot(mat_hi[rows, :], w_cat[...]))
                part = part + dot(mat_lo[rows, :], w_cat[:, :PLANS])
                for k in range(PAIR // BLK):
                    b = g * (PAIR // BLK) + k
                    at = 2 * k * BLK
                    first = warped(warp[b], part[at : at + BLK])
                    second = warped(warp[PER + b], part[at + BLK : at + 2 * BLK])
                    out_buf[h, pl.ds(b, NDEV, stride=PER), :] = jnp.where(left(BLK), first, second)

            send_all(
                lambda to: out_buf.at[h, pl.ds(to * PER, PER)],
                in_buf.at[it, h, pl.ds(me * PER, PER)],
                out_ss.at[h],
                out_rs.at[it, h],
            )

        @pl.loop(0, PARTS)
        def _(h):
            pl.when(it == 0)(lambda: turn(h))
            wait(in_buf.at[it, h], out_rs.at[it, h])
            for b in range(PER):
                high, low = halves(in_buf[it, h, pl.ds(b, NDEV, stride=PER), :])
                in_cat[b * NDEV : (b + 1) * NDEV, :PLANS] = high
                in_cat[b * NDEV : (b + 1) * NDEV, PLANS:] = low
            near = left(TARGETS)
            total = jnp.where(
                near,
                joined(dot(gather_in[:, : PER * NDEV], in_cat[...])),
                joined(dot(gather_in[:, PER * NDEV :], in_cat[...])),
            )
            total = total + swapped(total)
            dose[h] = total
            high, low = halves(voxel_weight[...] * (total - target_dose[h]))
            adj_cat[:, :PLANS] = high
            adj_cat[:, PLANS:] = low
            for b in range(0, PER, PAIR // BLK):
                first = joined(dot(gather_t[b * NDEV : b * NDEV + PAIR, :], adj_cat[...]))
                second = (PER + b) * NDEV
                second = joined(dot(gather_t[second : second + PAIR, :], adj_cat[...]))
                both = jnp.where(left(PAIR), first, second)
                for k in range(PAIR // BLK):
                    back_buf[h, pl.ds(b + k, NDEV, stride=PER), :] = both[k * BLK : (k + 1) * BLK]
            send_all(
                lambda to: back_buf.at[h, pl.ds(to * PER, PER)],
                adj_buf.at[it, h, pl.ds(me * PER, PER)],
                back_ss.at[h],
                back_rs.at[it, h],
            )

        def deposit():
            for b in range(BLOCKS):
                rows = slice(b * NVOX, (b + 1) * NVOX)
                field_out[pl.ds(b, NVOX, stride=BLOCKS), :] = jnp.where(
                    left(NVOX), dose[0, rows, :], dose[1, rows, :]
                )
            own = field_in.at[pl.ds(me * BLOCKS, BLOCKS)]
            for o in OFFSETS:
                if o // 32 != 2:
                    source = field_out.at[pl.ds(vox_of(index(o)) * BLOCKS, BLOCKS)]
                    send(source, own, field_ss, field_rs.at[o // 32], index(o))
            source = field_out.at[pl.ds(vox_of(me) * BLOCKS, BLOCKS)]
            pltpu.make_async_copy(source, own, field_rs.at[0]).start()

        def plane(dz):
            return pl.multiple_of(index(dz * 32) // 32 * PLANE, PLANE)

        def relay():
            wait(field_in.at[pl.ds(plane(3), PLANE)], field_rs.at[1])
            rows = field_in.at[pl.ds(plane(3), PLANE // 2)]
            send(rows, rows, relay_ss.at[0], relay_rs.at[0], index(32))
            wait(field_in.at[pl.ds(plane(1), PLANE)], field_rs.at[3])
            rows = field_in.at[pl.ds(plane(1) + PLANE // 2, PLANE // 2)]
            send(rows, rows, relay_ss.at[1], relay_rs.at[1], index(96))

        @pl.loop(0, PARTS)
        def _(h):
            wait(adj_buf.at[it, h], back_rs.at[it, h])
            for b in range(PER):
                high, low = halves(adj_buf[it, h, pl.ds(b, NDEV, stride=PER), :])
                value = jnp.concatenate([high, high, low], axis=0)
                near = left(BLK)
                for block, here in ((b, near), (PER + b, ~near)):
                    high, low = halves(jnp.where(here, dot(warp_t[block], value), 0.0))
                    rows = slice(place(block) * BLK, (place(block) + 1) * BLK)
                    la_cat[rows, :PLANS] = high
                    la_cat[rows, PLANS:] = low
            own = grad_in.at[it, h, pl.ds(chip * PACKED, PACKED)]
            order = (2, 1, 3, 0)

            def deliver(n):
                first = index(order[n] * 32) // 32
                layer = pl.multiple_of(first * (LAYER // 2), LAYER // 2)
                rows = pl.ds(layer, LAYER // 2)
                wait(pair_in.at[it, h, pl.ds(0, LAYER // 4)], pair_rs.at[it, h, n])
                grad_sum[h, rows, :] = grad[h, rows, :] + pair_in[it, h, rows, :]
                for o in CHIPS:
                    if o // 32 == order[n]:
                        to = index(o)
                        source = grad_sum.at[h, pl.ds(to * PACKED, PACKED)]
                        send(source, own, grad_ss.at[h], grad_rs.at[it, h], to)

            for n, dz in enumerate(order):
                first = index(dz * 32) // 32
                rows = pl.ds(pl.multiple_of(first * LAYER, LAYER), LAYER)
                part = joined(dot(tra_hi[rows, :], la_cat[...]))
                part = part + dot(tra_lo[rows, :], la_cat[:, :PLANS])
                flat[...] = part + swapped(part)
                even = flat[pl.ds(0, LAYER // 2, stride=2), :]
                odd = flat[pl.ds(1, LAYER // 2, stride=2), :]
                rows = pl.ds(pl.multiple_of(first * (LAYER // 2), LAYER // 2), LAYER // 2)
                grad[h, rows, :] = jnp.where(left(LAYER // 2), even, odd)
                for k in range(NVOX // 2):
                    device = first * NVOX + 2 * k + partner % 2
                    rows = pl.ds(device * PACKED, PACKED)
                    send(
                        grad.at[h, rows],
                        pair_in.at[it, h, rows],
                        pair_ss.at[h],
                        pair_rs.at[it, h, n],
                        partner,
                    )
                if n > 0:
                    deliver(n - 1)
                if n == DEPOSIT:
                    pl.when((it == ITERS - 1) & (h == 0))(deposit)
            pl.when((it == ITERS - 1) & (h == PARTS - 1))(relay)
            deliver(len(order) - 1)
            source = grad_sum.at[h, pl.ds(me * PACKED, PACKED)]
            pltpu.make_async_copy(source, own, grad_rs.at[it, h]).start()

        @pl.when(it == ITERS - 1)
        def _():
            wait(field_in.at[pl.ds(plane(0), PLANE)], field_rs.at[0])
            for k in range(2):
                half = field_in.at[pl.ds(plane(2) + k * (PLANE // 2), PLANE // 2)]
                wait(half, relay_rs.at[k])
            for b in range(BLOCKS):
                field[b * BLK : (b + 1) * BLK, :] = field_in[pl.ds(b, NDEV, stride=BLOCKS), :]
            stored.start()

        @pl.loop(0, PARTS)
        def _(h):
            wait(grad_in.at[it, h], grad_rs.at[it, h])
            for r in range(PACKED):
                total = jnp.sum(
                    grad_in[it, h, pl.ds(r, NCHIP, stride=PACKED), :], axis=0, keepdims=True
                )
                w_own[it + 1, h, r : r + 1, :] = jnp.maximum(
                    w_own[it, h, r : r + 1, :] - step_buf[pl.ds(h, 1), :] * total, 0.0
                )

            @pl.when(it < ITERS - 1)
            def _():
                share(it + 1, h)

        @pl.loop(0, PARTS)
        def _(h):
            wait(out_buf.at[h, pl.ds(0, (NDEV - 1) * PER)], out_ss.at[h])
            wait(back_buf.at[h, pl.ds(0, (NDEV - 1) * PER)], back_ss.at[h])
            wait(grad.at[h, pl.ds(0, (NCHIP - 1) * PACKED)], grad_ss.at[h])
            wait(grad.at[h, pl.ds(0, NCHIP * PACKED)], pair_ss.at[h])
            wait(w_buf.at[0, h, pl.ds(0, (NCHIP - 1) * PACKED)], w_ss.at[it, h])
            wait(w_buf.at[0, h, pl.ds(0, NCHIP * PACKED)], pass_ss.at[it, h])

    first, second = w_own[ITERS, 0, 0:PACKED, :], w_own[ITERS, 1, 0:PACKED, :]
    even = jnp.where(left(PACKED), first, swapped(second))
    odd = jnp.where(left(PACKED), swapped(first), second)
    for r in range(PACKED):
        new_weights[2 * r : 2 * r + 1, :] = even[r : r + 1, :]
        new_weights[2 * r + 1 : 2 * r + 2, :] = odd[r : r + 1, :]
    wait(info_in.at[pl.ds(0, NDEV - 1)], info_ss)
    wait(field_in.at[pl.ds(0, 3 * PLANE - BLOCKS)], field_ss)
    for k in range(2):
        wait(field_in.at[pl.ds(0, PLANE // 2)], relay_ss.at[k])
    stored.wait()


def finish(weights, field, new_weights, dose_field, small, large, in_sem, out_sem):
    pairs = [(weights, small, new_weights)]
    for n in range(4):
        rows = pl.ds(n * (ROWS // 4), ROWS // 4)
        pairs.append((field.at[rows], large.at[rows], dose_field.at[rows]))
    reads = [pltpu.make_async_copy(a, b, in_sem.at[n]) for n, (a, b, _) in enumerate(pairs)]
    writes = [pltpu.make_async_copy(b, c, out_sem.at[n]) for n, (_, b, c) in enumerate(pairs)]
    for read in reads:
        read.start()
    for read, write in zip(reads, writes):
        read.wait()
        write.start()
    for write in writes:
        write.wait()


def per_device(
    influence,
    weights,
    warp_tiles,
    owners,
    owner_slot,
    tile_index,
    structure,
    prescribed,
    importance,
    step_size,
):
    vmem = pl.BlockSpec(memory_space=pltpu.VMEM)
    smem = pl.BlockSpec(memory_space=pltpu.SMEM)
    hbm = pl.BlockSpec(memory_space=pl.ANY)
    dma = pltpu.SemaphoreType.DMA
    scratch = [
        pltpu.VMEM((4, LOAD, SPOTS), F32),
        pltpu.VMEM((ROWS, SPOTS), BF16),
        pltpu.VMEM((ROWS, SPOTS), BF16),
        pltpu.VMEM((SPOTS, ROWS), BF16),
        pltpu.VMEM((SPOTS, ROWS), BF16),
        pltpu.VMEM((NTILE, BLK, BLK), F32),
        pltpu.VMEM((BLOCKS, BLK, 3 * BLK), BF16),
        pltpu.VMEM((BLOCKS, BLK, 3 * BLK), BF16),
        pltpu.VMEM((BLK, BLK), F32),
        pltpu.VMEM((BLK, BLK), F32),
        pltpu.VMEM((TARGETS, SOURCES), BF16),
        pltpu.VMEM((SOURCES, TARGETS), BF16),
        pltpu.VMEM((ITERS, PARTS, SPOTS // 2, PLANS), F32),
        pltpu.VMEM((SPOTS, PLANS), F32),
        pltpu.VMEM((SPOTS, 2 * PLANS), BF16),
        pltpu.VMEM((ITERS + 1, PARTS, 8, PLANS), F32),
        pltpu.VMEM((8, PLANS), F32),
        pltpu.VMEM((PARTS, NDEV * PER, PLANS), F32),
        pltpu.VMEM((ITERS, PARTS, NDEV * PER, PLANS), F32),
        pltpu.VMEM((NDEV * PER, 2 * PLANS), BF16),
        pltpu.VMEM((PARTS, TARGETS, PLANS), F32),
        pltpu.VMEM((PARTS, TARGETS, PLANS), F32),
        pltpu.VMEM((TARGETS, PLANS), F32),
        pltpu.VMEM((TARGETS, 2 * PLANS), BF16),
        pltpu.VMEM((PARTS, NDEV * PER, PLANS), F32),
        pltpu.VMEM((ITERS, PARTS, NDEV * PER, PLANS), F32),
        pltpu.VMEM((ROWS, 2 * PLANS), BF16),
        pltpu.VMEM((LAYER, PLANS), F32),
        pltpu.VMEM((PARTS, SPOTS // 2, PLANS), F32),
        pltpu.VMEM((ITERS, PARTS, SPOTS // 2, PLANS), F32),
        pltpu.VMEM((PARTS, SPOTS // 2, PLANS), F32),
        pltpu.VMEM((ITERS, PARTS, NCHIP * PACKED, PLANS), F32),
        pltpu.VMEM((NVOX * BLOCKS, PLANS), F32),
        pltpu.VMEM((NDEV * BLOCKS, PLANS), F32),
        pltpu.VMEM((ROWS, PLANS), F32),
        dma((4,)),
        dma,
        dma,
        dma,
        dma((ITERS, PARTS)),
        dma((ITERS, PARTS)),
        dma((ITERS, PARTS)),
        dma((ITERS, PARTS)),
        dma((PARTS,)),
        dma((ITERS, PARTS)),
        dma((PARTS,)),
        dma((ITERS, PARTS)),
        dma((PARTS,)),
        dma((ITERS, PARTS, 4)),
        dma((PARTS,)),
        dma((ITERS, PARTS)),
        dma,
        dma((4,)),
        dma((2,)),
        dma((2,)),
    ]
    outs = (
        jax.ShapeDtypeStruct((OWN, PLANS), F32),
        jax.ShapeDtypeStruct((ROWS, PLANS), F32),
    )
    final_weights, field = pl.pallas_call(
        kernel,
        out_shape=outs,
        in_specs=[smem, smem, hbm, vmem, hbm, vmem, vmem, vmem, vmem, vmem],
        out_specs=(vmem, hbm),
        scratch_shapes=scratch,
        compiler_params=pltpu.CompilerParams(
            collective_id=0, has_side_effects=True, vmem_limit_bytes=67043328
        ),
    )(
        tile_index,
        importance.reshape(1, NSTRUCT),
        influence,
        weights,
        warp_tiles,
        owners.reshape(1, BLOCKS),
        owner_slot,
        structure.reshape(BLOCKS, BLK),
        prescribed,
        step_size.reshape(1, PLANS),
    )
    return pl.pallas_call(
        finish,
        out_shape=outs,
        in_specs=[hbm, hbm],
        out_specs=(hbm, hbm),
        scratch_shapes=[
            pltpu.VMEM((OWN, PLANS), F32),
            pltpu.VMEM((ROWS, PLANS), F32),
            dma((5,)),
            dma((5,)),
        ],
    )(final_weights, field)


def solution(mesh):
    split = Mesh(mesh.devices.reshape(SIZES), AXES)
    both = P("z", VOX)
    placed = (
        P("z", VOX, None),
        P(AXES, None),
        P(),
        P("z", VOX, None),
        both,
        both,
        P(VOX),
        P(),
        P(),
        P(),
    )
    return jax.shard_map(
        per_device,
        mesh=split,
        in_specs=placed,
        out_specs=(P(AXES, None), P(VOX, None)),
        check_vma=False,
    )
```
